128 devices in a mesh: fit: 8 (over x, core), ao: 16 (over z, y).
Axes of the slice: x: 4, y: 4, z: 4, core: 2. Of those that a mesh axis runs over, the one named last changes fastest.
Arguments:
- three_index: bfloat16 [64, 128, 128, 1024], P('ao', None, None, 'fit'), may hold values from -384 to 384
- occ_coeff: bfloat16 [128, 128, 128], P(('fit', 'ao')), may hold values from -0.005859375 to 0.005859375
- occ_owner: int32 [2], replicated, may hold values from 0 to 127
- screen: int32 [64, 8], P('ao', 'fit'), may hold values 0 or 1
- tile_owner: int32 [2048, 1], P(('fit', 'ao')), may hold values from 0 to 15; in each aligned block of 16 rows (0 to 15, 16 to 31, ...) at most 2 rows name the same one
- tile_slot: int32 [2048], P(('fit', 'ao')), may hold values from 0 to 15
Outputs:
- fock: float32 [256, 128, 128], P(('fit', 'ao'))
The draws below stay inside these ranges and needn't reach their ends.
Inputs may be any that keep to these rules, and one draw needn't show every extreme that they name: `tile_owner`: among the 16 tiles of one device, at most 2 name the same owner; some device sends exactly 2 tiles to some owner.
All inputs are finite; a program needn't handle non-finite values. No bound on the sum of `screen` on one device may be relied on, other than what follows from the above.
Results may differ from the reference program's by a relative error of at most 0.0003.
Values may be sent and summed in bfloat16 or wider, within the bound.
A program may use at most 192 MiB of HBM per device.

```python
import math
import jax
import jax.numpy as jnp
import numpy as np
from jax import lax

BLK = 128
OCC = 128
NU = 128
MUB = 4
CAP = 2
FT_DEV = 2
TILES = 16
FT = 16
MBLOCKS = 64
N_FIT = 8
N_AO = 16
DEVICES = 128


def draw_three_index(key, part):

    def one_group(group):
        base = jax.random.fold_in(key, group)
        k_base = jax.random.fold_in(base, 0)
        k_mix = jax.random.fold_in(base, 1)
        k_cross = jax.random.fold_in(base, 2)
        k_common = jax.random.fold_in(base, 5)
        k_weight = jax.random.fold_in(base, 6)
        shape = (MUB, NU, BLK, BLK * N_FIT)
        rough = jax.random.randint(k_base, shape, -15, 16).astype(jnp.float32)
        factor = 1.0 / 384.0
        identity = jnp.eye(BLK, dtype=jnp.int32)
        common = jax.random.randint(k_common, (MUB, 1, BLK), -1, 2)
        weights = jax.random.randint(k_weight, (MUB, BLK, 1), -2, 3)
        mixing = 2 * identity[None] + jax.random.randint(k_mix, (MUB, BLK, BLK), -2, 3) + weights * common
        mixing = mixing.astype(jnp.float32)
        ident_blocks = jnp.eye(MUB, dtype=jnp.int32)
        cross = (2 * ident_blocks[:, :, None] + jax.random.randint(k_cross, (MUB, MUB, BLK), -1, 2)).astype(jnp.float32)
        mixed = jnp.einsum('jmn,jvnp->jvmp', mixing, rough, precision=lax.Precision.HIGHEST)
        mixed = jnp.einsum('jkm,kvmp->jvmp', cross, mixed, precision=lax.Precision.HIGHEST)
        return (mixed * factor).astype(jnp.bfloat16)
    groups = lax.map(one_group, jnp.arange(N_AO, dtype=jnp.int32))
    return groups.reshape(MBLOCKS, NU, BLK, BLK * N_FIT)


def plant(entries, stream_key, least, high):
    spot = [jax.random.randint(jax.random.fold_in(stream_key, axis), (), 0, length) for axis, length in enumerate(entries.shape)]
    widest = entries.shape.index(max(entries.shape))
    neighbour = spot[:widest] + [(spot[widest] + 1) % entries.shape[widest]] + spot[widest + 1:]
    return entries.at[tuple(spot)].set(least).at[tuple(neighbour)].set(high)


def shard_levels(key, shape, pieces, least, largest):
    gain, own = 1.0, jax.random.fold_in(key, 6)
    for axis_at, shards_of in pieces:
        draws = jnp.exp(jax.random.uniform(jax.random.fold_in(own, axis_at), (shards_of,), jnp.float32, least / len(pieces), largest / len(pieces)))
        gain = gain * jnp.repeat(draws, shape[axis_at] // shards_of).reshape([-1 if axis == axis_at else 1 for axis in range(len(shape))])
    return gain


def shared_out(own_key, own, number, rows, number_of, top, most, lean):
    ranking = jax.random.permutation(own_key, number_of)
    packed, usual = shares(number_of, rows * top, most, lean, True), shares(number_of, rows * top, most, lean, False)
    places = jnp.arange(number_of)

    def named(sizes, rotation):
        used = int((sizes > 0).sum())
        fixed = max(1, used // 4)
        shifted = fixed + (places - fixed + rotation * (used - fixed)) % max(1, number_of - fixed)
        return jnp.zeros((number_of,), jnp.int32).at[ranking[jnp.where(places < fixed, places, shifted)]].set(jnp.asarray(sizes, jnp.int32))

    sizes = jnp.where(number % 4 == 0, named(packed, number // 4), named(usual, number - number // 4 - 1))
    mixed = jax.random.permutation(jax.random.fold_in(own, 3), number_of)
    giver, taker = mixed[0:number_of // 2 * 2:2], mixed[1:number_of // 2 * 2:2]
    margin = jnp.minimum(sizes[giver] - 1, most - sizes[taker]) // 2
    margin = jnp.where((giver == ranking[0]) | (taker == ranking[0]) | (sizes[taker] == 0), 0, jnp.maximum(margin, 0))
    shifted = jax.random.randint(jax.random.fold_in(own, 4), (number_of // 2,), 0, 1 << 20) % (margin + 1)
    sizes = sizes.at[giver].add(-shifted).at[taker].add(shifted)
    members = jnp.searchsorted(jnp.cumsum(sizes), jnp.arange(rows * top), side="right").astype(jnp.int32)
    listing = members.reshape(top, rows).T
    listing = listing[jax.random.permutation(jax.random.fold_in(own, 1), rows)]
    rotation = jax.random.randint(jax.random.fold_in(own, 2), (rows, 1), 0, top)
    return jnp.take_along_axis(listing, (jnp.arange(top)[None, :] + rotation) % top, axis=1)


def shares(count, total, reach, skew, full):
    loads = [(1 << 20) // math.isqrt(standing ** skew) + 1 for standing in range(1, count + 1)]
    largest = reach if full else min(reach, max(-(-total // count), total * loads[0] // sum(loads)))
    least = 1 if total - largest >= count - 1 else 0
    holding, spare = [largest] + [least] * (count - 1), total - largest - least * (count - 1)
    while spare > 0:
        movable = [i for i in range(1, count) if holding[i] < largest] or [i for i in range(1, count) if holding[i] < reach]
        pool, remaining = sum([loads[i] for i in movable]), spare
        for i in movable:
            extra = min(reach - holding[i], max(1, remaining * loads[i] // pool), spare)
            holding[i] = holding[i] + extra
            spare = spare - extra
    return np.array(holding)


def noise(key, extent, width, limit, pieces=(), held_as=jnp.bfloat16):
    entries = jax.random.normal(key, extent, jnp.float32) * width
    if len(pieces) > 0:
        entries = shard_levels(key, extent, pieces, -0.22, 0.18) * entries
    return jnp.clip(entries, min=-limit, max=limit).astype(held_as)


def setup_inputs(seed: int = 0) -> dict:
    streams_of = jax.random.split(jax.random.key(seed), 7)
    three_index = draw_three_index(jax.random.fold_in(streams_of[6], 71), 0)
    occ_coeff = noise(streams_of[1], (DEVICES, NU, OCC), (NU * 8192) ** -0.5, 0.005859375, ((0, 128),))
    occ_owner = jax.random.randint(streams_of[2], (2,), 0, DEVICES).astype(jnp.int32)
    screen = plant((jax.random.randint(streams_of[3], (MBLOCKS, N_FIT), 0, 4) < 3).astype(jnp.int32), jax.random.fold_in(streams_of[3], 1), 0, 1)
    tile_owner_keys = jax.random.split(jax.random.fold_in(streams_of[4], 1), (DEVICES * TILES) // TILES)
    tile_owner_turns = jax.random.permutation(jax.random.fold_in(streams_of[4], 3), (DEVICES * TILES) // TILES)
    tile_owner = jax.vmap(lambda own, number: shared_out(jax.random.fold_in(streams_of[4], 2), own, number, TILES, N_AO, 1, CAP, 2))(tile_owner_keys, tile_owner_turns).reshape((DEVICES * TILES, 1))
    tile_slot = plant(jax.random.randint(streams_of[5], (DEVICES * TILES,), 0, FT), jax.random.fold_in(streams_of[5], 1), 0, FT - 1).astype(jnp.int32)
    return dict(three_index=three_index, occ_coeff=occ_coeff, occ_owner=occ_owner, screen=screen, tile_owner=tile_owner, tile_slot=tile_slot)


def reference(three_index, occ_coeff, occ_owner, screen, tile_owner, tile_slot):
    coeff = jnp.concatenate([occ_coeff[occ_owner[0]], occ_coeff[occ_owner[1]]], axis=1).astype(jnp.float32)
    owner_all = tile_owner[:, 0]

    def one_device(device):
        fit_index = (device // N_AO).astype(jnp.int32)
        ao_index = (device % N_AO).astype(jnp.int32)
        zero = jnp.int32(0)
        block = lax.dynamic_slice(three_index, (ao_index * MUB, zero, zero, fit_index * BLK), (MUB, NU, BLK, BLK)).astype(jnp.float32)
        half = jnp.einsum('jvmp,vi->jmpi', block, coeff, precision=lax.Precision.HIGHEST)
        mask = lax.dynamic_slice(screen, (ao_index * MUB, fit_index), (MUB, 1)).astype(jnp.float32)
        half = (half * mask[:, 0][:, None, None, None]).astype(jnp.bfloat16)
        half = lax.optimization_barrier(half).astype(jnp.float32)
        flat = half.reshape(MUB, BLK, BLK * 2 * OCC)
        gram = jnp.einsum('jmx,knx->jkmn', flat, flat, precision=lax.Precision.HIGHEST).reshape(TILES, BLK, BLK)
        owners = lax.dynamic_slice(owner_all, (device * TILES,), (TILES,)).astype(jnp.int32)
        slots = lax.dynamic_slice(tile_slot, (device * TILES,), (TILES,)).astype(jnp.int32)
        glob = (slots // FT_DEV) * (N_AO * FT_DEV) + owners * FT_DEV + slots % FT_DEV
        return gram, glob

    def add_device(device, fock):
        gram, glob = one_device(device)
        return fock.at[glob].add(gram)

    fock = jnp.zeros((DEVICES * FT_DEV, BLK, BLK), jnp.float32)
    return lax.fori_loop(jnp.int32(0), jnp.int32(DEVICES), add_device, fock)
```

```python
import functools

import jax
import jax.numpy as jnp
from jax import lax
from jax.experimental import pallas as pl
from jax.experimental.pallas import tpu as pltpu
from jax.sharding import PartitionSpec as P

MESH = pl.DeviceIdType.MESH
NF = 8
NA = 16
SIDE = 4
CAP = 2
SLOTS = 16
W = 128
CHUNKS = 4
ROWS = W // CHUNKS


def ao_peer(ao, step, sign):
    z, y = ao // SIDE, ao % SIDE
    dz, dy = step // SIDE, step % SIDE
    return (z + SIDE + sign * dz) % SIDE * SIDE + (y + SIDE + sign * dy) % SIDE


def greet():
    fit, ao = lax.axis_index("fit"), lax.axis_index("ao")
    barrier = pltpu.get_barrier_semaphore()

    def to_fit(i, carry):
        pl.semaphore_signal(barrier, inc=1, device_id=((fit + i) % NF, ao), device_id_type=MESH)
        return carry

    def to_ao(i, carry):
        pl.semaphore_signal(barrier, inc=1, device_id=(fit, ao_peer(ao, i, 1)), device_id_type=MESH)
        return carry

    lax.fori_loop(1, NF, to_fit, 0)
    lax.fori_loop(1, NA, to_ao, 0)
    pl.semaphore_wait(barrier, NF - 1 + NA - 1)
    return fit, ao


def each(start, stop, body):
    def step(i, carry):
        body(i)
        return carry

    lax.fori_loop(start, stop, step, 0)


def coeff_kernel(owner_ref, occ_ref, out_ref, own, first, piece, second, whole, done, s1, r1, s2, r2, s3, r3):
    fit, ao = greet()
    me = fit * NA + ao
    rows = W // 4
    for which in range(2):
        keep = jnp.where(owner_ref[which] == me, 1.0, 0.0).astype(jnp.float32)
        block = (occ_ref[...].astype(jnp.float32) * keep).astype(jnp.bfloat16)
        own[pl.ds(which * 4, 4)] = block.reshape(4, rows, W)

    def hop1(i):
        peer = (fit + i) % NF
        return pltpu.make_async_remote_copy(
            src_ref=own.at[peer], dst_ref=first.at[i], send_sem=s1.at[i], recv_sem=r1.at[i],
            device_id=(peer, ao), device_id_type=MESH)

    def hop2(i):
        return pltpu.make_async_remote_copy(
            src_ref=piece, dst_ref=second.at[i], send_sem=s2.at[i], recv_sem=r2.at[i],
            device_id=(fit, ao_peer(ao, i, 1)), device_id_type=MESH)

    def hop3(i):
        return pltpu.make_async_remote_copy(
            src_ref=whole, dst_ref=done.at[i], send_sem=s3.at[i], recv_sem=r3.at[i],
            device_id=((fit + i) % NF, ao), device_id_type=MESH)

    each(1, NF, lambda i: hop1(i).start())
    each(1, NF, lambda i: hop1(i).wait_recv())
    total = own[fit].astype(jnp.float32)
    for i in range(1, NF):
        total = total + first[i].astype(jnp.float32)
    piece[...] = total.astype(jnp.bfloat16)
    each(1, NA, lambda i: hop2(i).start())
    each(1, NA, lambda i: hop2(i).wait_recv())
    for i in range(1, NA):
        total = total + second[i].astype(jnp.float32)
    whole[...] = total.astype(jnp.bfloat16)
    each(1, NF, lambda i: hop3(i).start())
    out_ref[fit] = whole[...]
    each(1, NF, lambda i: hop3(i).wait_recv())

    def put(i):
        out_ref[(fit + NF - i) % NF] = done[i]

    each(1, NF, put)
    each(1, NF, lambda i: hop1(i).wait_send())
    each(1, NA, lambda i: hop2(i).wait_send())
    each(1, NF, lambda i: hop3(i).wait_send())


def gather_coeff(occ_owner, occ):
    rows = W // 4
    piece = (rows, W)
    out = pl.pallas_call(
        coeff_kernel,
        out_shape=jax.ShapeDtypeStruct((NF, rows, W), jnp.bfloat16),
        in_specs=[pl.BlockSpec(memory_space=pltpu.SMEM), pl.BlockSpec(memory_space=pltpu.VMEM)],
        out_specs=pl.BlockSpec(memory_space=pltpu.VMEM),
        scratch_shapes=[
            pltpu.VMEM((NF,) + piece, jnp.bfloat16),
            pltpu.VMEM((NF,) + piece, jnp.bfloat16),
            pltpu.VMEM(piece, jnp.bfloat16),
            pltpu.VMEM((NA,) + piece, jnp.bfloat16),
            pltpu.VMEM(piece, jnp.bfloat16),
            pltpu.VMEM((NF,) + piece, jnp.bfloat16),
            pltpu.SemaphoreType.DMA((NF,)), pltpu.SemaphoreType.DMA((NF,)),
            pltpu.SemaphoreType.DMA((NA,)), pltpu.SemaphoreType.DMA((NA,)),
            pltpu.SemaphoreType.DMA((NF,)), pltpu.SemaphoreType.DMA((NF,)),
        ],
        compiler_params=pltpu.CompilerParams(collective_id=0, has_side_effects=True),
        name="coeff",
    )(occ_owner, occ)
    return out.reshape(2, W, W)


def fock_kernel(tab_ref, slot_ref, gram_ref, out_ref, send, recv, bsend, brecv, sa, ra, sb, rb):
    fit, ao = greet()

    def hop_a(c, i):
        return pltpu.make_async_remote_copy(
            src_ref=send.at[c, i], dst_ref=recv.at[c, i], send_sem=sa.at[c, i], recv_sem=ra.at[c, i],
            device_id=(fit, ao_peer(ao, i, 1)), device_id_type=MESH)

    def hop_b(c, i):
        peer = (fit + i) % NF
        return pltpu.make_async_remote_copy(
            src_ref=bsend.at[c, peer], dst_ref=brecv.at[c, i], send_sem=sb.at[c, i], recv_sem=rb.at[c, i],
            device_id=(peer, ao), device_id_type=MESH)

    def fill(c, i, where_to):
        owner = ao_peer(ao, i, 1)
        for r in range(CAP):
            tile = tab_ref[owner * CAP + r]
            where_to[c, i, pl.ds(r * ROWS, ROWS)] = gram_ref[tile, pl.ds(c * ROWS, ROWS)]
            slot = slot_ref[owner * CAP + r].astype(jnp.float32)
            where_to[c, i, pl.ds(CAP * ROWS + r * 8, 8)] = jnp.full((8, W), slot, jnp.float32)

    for c in range(CHUNKS):
        def push(i, c=c):
            fill(c, i, send)
            hop_a(c, i).start()

        each(1, NA, push)
        fill(c, 0, recv)

    places = lax.broadcasted_iota(jnp.int32, (SLOTS, 8, W), 0).astype(jnp.float32)
    for c in range(CHUNKS):
        each(1, NA, lambda i, c=c: hop_a(c, i).wait_recv())

        def band(b, c=c):
            def add(i, acc):
                for r in range(CAP):
                    tile = recv[c, i, pl.ds(r * ROWS + b * 8, 8)]
                    slot = recv[c, i, pl.ds(CAP * ROWS + r * 8, 8)]
                    acc = acc + jnp.where(slot[None] == places, tile[None], 0.0)
                return acc

            acc = lax.fori_loop(0, NA, add, jnp.zeros((SLOTS, 8, W), jnp.float32))
            bsend[c, :, :, pl.ds(b * 8, 8)] = acc.reshape(NF, 2, 8, W)

        each(0, ROWS // 8, band)
        each(1, NF, lambda i, c=c: hop_b(c, i).start())

    for c in range(CHUNKS):
        each(1, NF, lambda i, c=c: hop_b(c, i).wait_recv())
        total = bsend[c, fit]
        for i in range(1, NF):
            total = total + brecv[c, i]
        out_ref[:, pl.ds(c * ROWS, ROWS)] = total

    for c in range(CHUNKS):
        each(1, NA, lambda i, c=c: hop_a(c, i).wait_send())
        each(1, NF, lambda i, c=c: hop_b(c, i).wait_send())


def spread_fock(tab, slot, gram):
    return pl.pallas_call(
        fock_kernel,
        out_shape=jax.ShapeDtypeStruct((2, W, W), jnp.float32),
        in_specs=[pl.BlockSpec(memory_space=pltpu.SMEM), pl.BlockSpec(memory_space=pltpu.SMEM),
                  pl.BlockSpec(memory_space=pltpu.VMEM)],
        out_specs=pl.BlockSpec(memory_space=pltpu.VMEM),
        scratch_shapes=[
            pltpu.VMEM((CHUNKS, NA, CAP * (ROWS + 8), W), jnp.float32),
            pltpu.VMEM((CHUNKS, NA, CAP * (ROWS + 8), W), jnp.float32),
            pltpu.VMEM((CHUNKS, NF, 2, ROWS, W), jnp.float32),
            pltpu.VMEM((CHUNKS, NF, 2, ROWS, W), jnp.float32),
            pltpu.SemaphoreType.DMA((CHUNKS, NA)), pltpu.SemaphoreType.DMA((CHUNKS, NA)),
            pltpu.SemaphoreType.DMA((CHUNKS, NF)), pltpu.SemaphoreType.DMA((CHUNKS, NF)),
        ],
        compiler_params=pltpu.CompilerParams(
            collective_id=1, has_side_effects=True, vmem_limit_bytes=32 << 20),
        name="fock",
    )(tab, slot, gram)


def places_of(owners, slots):
    tiles = jnp.arange(16, dtype=jnp.int32)
    same = owners[:, None] == owners[None, :]
    rank = jnp.sum(jnp.where(same & (tiles[None, :] < tiles[:, None]), 1, 0), axis=1)
    place = owners * CAP + rank
    hit = place[None, :] == jnp.arange(NA * CAP, dtype=jnp.int32)[:, None]
    tab = jnp.sum(jnp.where(hit, tiles[None, :], 0), axis=1)
    slot = jnp.sum(jnp.where(hit, slots[None, :] + 1, 0), axis=1) - 1
    return tab.astype(jnp.int32), slot.astype(jnp.int32)


def on_device(three_index, occ_coeff, occ_owner, screen, tile_owner, tile_slot):
    pair = gather_coeff(occ_owner, occ_coeff[0])
    coeff = jnp.concatenate([pair[0], pair[1]], axis=1)
    mub = three_index.shape[0]
    width = three_index.shape[2]
    half = jnp.einsum("jvmp,vi->jmpi", three_index, coeff, preferred_element_type=jnp.float32)
    half = (half * screen[:, 0].astype(jnp.float32)[:, None, None, None]).astype(jnp.bfloat16)
    flat = half.reshape(mub, width, -1)
    gram = jnp.einsum("jmx,knx->jkmn", flat, flat, preferred_element_type=jnp.float32)
    gram = gram.reshape(mub * mub, width, width)
    tab, slot = places_of(tile_owner[:, 0], tile_slot)
    return spread_fock(tab, slot, gram)


def solution(mesh):
    in_specs = (
        P("ao", None, None, "fit"),
        P(("fit", "ao"), None, None),
        P(),
        P("ao", "fit"),
        P(("fit", "ao"), None),
        P(("fit", "ao")),
    )
    out_specs = P(("fit", "ao"), None, None)
    return jax.shard_map(
        on_device, mesh=mesh, in_specs=in_specs, out_specs=out_specs, check_vma=False
    )
```

```python
import jax
import jax.numpy as jnp
from jax import lax
from jax.experimental import pallas as pl
from jax.experimental.pallas import tpu as pltpu
from jax.sharding import PartitionSpec as P

MESH = pl.DeviceIdType.MESH
F32, BF16 = jnp.float32, jnp.bfloat16
NF, NA, SIDE = 8, 16, 4
MUB, TILES, SLOTS, CAP = 4, 16, 16, 2
W = 128
ORB = 2 * W
PIECE = W // 4
CHUNKS = 2
ROWS = W // CHUNKS
BAND = 32
BANDS = W // BAND
DEEP = 32
NT = (((1,), (1,)), ((), ()))


def each(start, stop, body):
    def step(i, carry):
        body(i)
        return carry

    lax.fori_loop(start, stop, step, 0)


def whole_kernel(
    owner_ref, screen_ref, tile_owner_ref, tile_slot_ref, occ_ref, three_ref, out_ref,
    three, half, acc, gram, own, first, piece, second, both, done, coeff,
    slots_out, slots_in, send, recv, bsend, brecv, tab, qtab,
    load, s1, r1, s2, r2, s3, r3, sm, rm, sa, ra, sb, rb,
):
    fit, ao = lax.axis_index("fit"), lax.axis_index("ao")
    me = fit * NA + ao
    z, y = lax.div(ao, SIDE), lax.rem(ao, SIDE)

    def fit_peer(i):
        return lax.rem(fit + i, NF)

    def ao_peer(i):
        return lax.rem(z + lax.div(i, SIDE), SIDE) * SIDE + lax.rem(y + lax.rem(i, SIDE), SIDE)

    def fetch(u):
        j, b = lax.div(u, BANDS), lax.rem(u, BANDS)
        rows = pl.ds(pl.multiple_of(b * BAND, BAND), BAND)
        return pltpu.make_async_copy(three_ref.at[j, :, rows], three.at[j, :, rows], load.at[u])

    each(0, MUB * BANDS, lambda u: fetch(u).start())

    barrier = pltpu.get_barrier_semaphore()

    def greet_fit(i):
        pl.semaphore_signal(barrier, inc=1, device_id=(fit_peer(i), ao), device_id_type=MESH)

    def greet_ao(i):
        pl.semaphore_signal(barrier, inc=1, device_id=(fit, ao_peer(i)), device_id_type=MESH)

    each(1, NF, greet_fit)
    each(1, NA, greet_ao)

    flipped = occ_ref[...].astype(F32).T
    for which in range(2):
        keep = jnp.where(owner_ref[which] == me, 1.0, 0.0).astype(F32)
        own[pl.ds(which * 4, 4)] = (flipped * keep).astype(BF16).reshape(4, PIECE, W)

    pl.semaphore_wait(barrier, NF - 1 + NA - 1)

    def hop1(i):
        peer = fit_peer(i)
        return pltpu.make_async_remote_copy(
            src_ref=own.at[peer], dst_ref=first.at[i], send_sem=s1.at[i], recv_sem=r1.at[i],
            device_id=(peer, ao), device_id_type=MESH)

    def hop2(i):
        return pltpu.make_async_remote_copy(
            src_ref=piece, dst_ref=second.at[i], send_sem=s2.at[i], recv_sem=r2.at[i],
            device_id=(fit, ao_peer(i)), device_id_type=MESH)

    def hop3(i):
        return pltpu.make_async_remote_copy(
            src_ref=both, dst_ref=done.at[i], send_sem=s3.at[i], recv_sem=r3.at[i],
            device_id=(fit_peer(i), ao), device_id_type=MESH)

    def hop_m(i):
        return pltpu.make_async_remote_copy(
            src_ref=slots_out.at[i], dst_ref=slots_in.at[i], send_sem=sm.at[i], recv_sem=rm.at[i],
            device_id=(fit, ao_peer(i)), device_id_type=MESH)

    def hop_a(c, i):
        return pltpu.make_async_remote_copy(
            src_ref=send.at[c, i], dst_ref=recv.at[c, i], send_sem=sa.at[c, i], recv_sem=ra.at[c, i],
            device_id=(fit, ao_peer(i)), device_id_type=MESH)

    def hop_b(c, i):
        peer = fit_peer(i)
        return pltpu.make_async_remote_copy(
            src_ref=bsend.at[c, peer], dst_ref=brecv.at[c, i], send_sem=sb.at[c, i], recv_sem=rb.at[c, i],
            device_id=(peer, ao), device_id_type=MESH)

    each(1, NF, lambda i: hop1(i).start())

    def look(owner):
        count = jnp.int32(0)
        tile = [jnp.int32(0), jnp.int32(0)]
        slot = [jnp.int32(-1), jnp.int32(-1)]
        for t in range(TILES):
            hit = tile_owner_ref[t] == owner
            for r in range(CAP):
                here = jnp.logical_and(hit, count == r)
                tile[r] = jnp.where(here, t, tile[r])
                slot[r] = jnp.where(here, tile_slot_ref[t], slot[r])
            count = count + jnp.where(hit, 1, 0)
        for r in range(CAP):
            tab[owner * CAP + r] = tile[r]
            qtab[owner * CAP + r] = slot[r]

    each(0, NA, look)

    each(1, NF, lambda i: hop1(i).wait_recv())
    total = own[fit].astype(F32)
    for i in range(1, NF):
        total = total + first[i].astype(F32)
    piece[...] = total.astype(BF16)
    each(1, NA, lambda i: hop2(i).start())

    def tell(i, where_to):
        owner = ao_peer(i)
        for r in range(CAP):
            slot = qtab[owner * CAP + r].astype(F32)
            where_to[i, pl.ds(r * 8, 8)] = jnp.full((8, W), slot, F32)

    each(1, NA, lambda i: tell(i, slots_out))
    tell(jnp.int32(0), slots_in)

    each(1, NA, lambda i: hop2(i).wait_recv())
    for i in range(1, NA):
        total = total + second[i].astype(F32)
    both[...] = total.astype(BF16)
    each(1, NF, lambda i: hop3(i).start())
    each(1, NA, lambda i: hop_m(i).start())
    coeff[fit] = both[...]
    each(1, NF, lambda i: hop3(i).wait_recv())

    def put(i):
        coeff[lax.rem(fit + NF - i, NF)] = done[i]

    each(1, NF, put)

    def product(u):
        fetch(u).wait()
        j, b = lax.div(u, BANDS), lax.rem(u, BANDS)
        rows = pl.ds(pl.multiple_of(b * BAND, BAND), BAND)
        block = jnp.swapaxes(three[j, :, rows, :], 0, 1)
        orbitals = coeff[...].reshape(ORB, W)
        parts = []
        for m in range(0, BAND, 2):
            pair = jnp.concatenate([block[m], block[m + 1]], 1)
            r = jnp.dot(orbitals, pair, preferred_element_type=F32).astype(BF16)
            parts += [r[:, :W], r[:, W:]]
        half[j, :, rows, :] = jnp.swapaxes(jnp.stack(parts, 0), 0, 1)

    each(0, MUB * BANDS, product)

    def rows_of(first_orbital, lo, n):
        return jnp.concatenate(
            [half[:, first_orbital + v, lo:lo + n, :].reshape(MUB * n, W) for v in range(DEEP)], 1)

    def fill(c, i, where_to):
        owner = ao_peer(i)
        for r in range(CAP):
            where_to[c, i, pl.ds(r * ROWS, ROWS)] = gram[c, tab[owner * CAP + r]]

    for c in range(CHUNKS):
        acc[...] = jnp.zeros_like(acc)

        def deep(i, c=c):
            acc[...] += lax.dot_general(
                rows_of(i * DEEP, c * ROWS, ROWS), rows_of(i * DEEP, 0, W), NT,
                preferred_element_type=F32)

        each(0, ORB // DEEP, deep)
        for j in range(MUB):
            for k in range(MUB):
                keep = (screen_ref[j] * screen_ref[k]).astype(F32)
                gram[c, j * MUB + k] = acc[j * ROWS:(j + 1) * ROWS, k * W:(k + 1) * W] * keep

        def push(i, c=c):
            fill(c, i, send)
            hop_a(c, i).start()

        each(1, NA, push)
        fill(c, jnp.int32(0), recv)

    each(1, NA, lambda i: hop_m(i).wait_recv())
    places = lax.broadcasted_iota(jnp.int32, (SLOTS, 8, W), 0).astype(F32)
    for c in range(CHUNKS):
        each(1, NA, lambda i, c=c: hop_a(c, i).wait_recv())

        def band(b, c=c):
            def add(i, sums):
                for r in range(CAP):
                    tile = recv[c, i, pl.ds(r * ROWS + b * 8, 8)]
                    slot = slots_in[i, pl.ds(r * 8, 8)]
                    sums = sums + jnp.where(slot[None] == places, tile[None], 0.0)
                return sums

            sums = lax.fori_loop(0, NA, add, jnp.zeros((SLOTS, 8, W), F32))
            bsend[c, :, :, pl.ds(b * 8, 8)] = sums.reshape(NF, 2, 8, W)

        each(0, ROWS // 8, band)
        each(1, NF, lambda i, c=c: hop_b(c, i).start())

    for c in range(CHUNKS):
        each(1, NF, lambda i, c=c: hop_b(c, i).wait_recv())
        sums = bsend[c, fit]
        for i in range(1, NF):
            sums = sums + brecv[c, i]
        out_ref[:, pl.ds(c * ROWS, ROWS)] = sums

    each(1, NF, lambda i: hop1(i).wait_send())
    each(1, NA, lambda i: hop2(i).wait_send())
    each(1, NF, lambda i: hop3(i).wait_send())
    each(1, NA, lambda i: hop_m(i).wait_send())
    for c in range(CHUNKS):
        each(1, NA, lambda i, c=c: hop_a(c, i).wait_send())
        each(1, NF, lambda i, c=c: hop_b(c, i).wait_send())


def on_device(three_index, occ_coeff, occ_owner, screen, tile_owner, tile_slot):
    smem = pl.BlockSpec(memory_space=pltpu.SMEM)
    vmem = pl.BlockSpec(memory_space=pltpu.VMEM)
    dma = pltpu.SemaphoreType.DMA
    part = (PIECE, W)
    return pl.pallas_call(
        whole_kernel,
        out_shape=jax.ShapeDtypeStruct((2, W, W), F32),
        in_specs=[smem, smem, smem, smem, vmem, pl.BlockSpec(memory_space=pl.ANY)],
        out_specs=vmem,
        scratch_shapes=[
            pltpu.VMEM((MUB, W, W, W), BF16),
            pltpu.VMEM((MUB, ORB, W, W), BF16),
            pltpu.VMEM((MUB * ROWS, MUB * W), F32),
            pltpu.VMEM((CHUNKS, TILES, ROWS, W), F32),
            pltpu.VMEM((NF,) + part, BF16),
            pltpu.VMEM((NF,) + part, BF16),
            pltpu.VMEM(part, BF16),
            pltpu.VMEM((NA,) + part, BF16),
            pltpu.VMEM(part, BF16),
            pltpu.VMEM((NF,) + part, BF16),
            pltpu.VMEM((NF,) + part, BF16),
            pltpu.VMEM((NA, CAP * 8, W), F32),
            pltpu.VMEM((NA, CAP * 8, W), F32),
            pltpu.VMEM((CHUNKS, NA, CAP * ROWS, W), F32),
            pltpu.VMEM((CHUNKS, NA, CAP * ROWS, W), F32),
            pltpu.VMEM((CHUNKS, NF, 2, ROWS, W), F32),
            pltpu.VMEM((CHUNKS, NF, 2, ROWS, W), F32),
            pltpu.SMEM((NA * CAP,), jnp.int32),
            pltpu.SMEM((NA * CAP,), jnp.int32),
            dma((MUB * BANDS,)),
            dma((NF,)), dma((NF,)), dma((NA,)), dma((NA,)), dma((NF,)), dma((NF,)),
            dma((NA,)), dma((NA,)),
            dma((CHUNKS, NA)), dma((CHUNKS, NA)), dma((CHUNKS, NF)), dma((CHUNKS, NF)),
        ],
        compiler_params=pltpu.CompilerParams(
            collective_id=0, has_side_effects=True, vmem_limit_bytes=60 << 20),
        name="exchange",
    )(occ_owner, screen[:, 0], tile_owner[:, 0], tile_slot, occ_coeff[0], three_index)


def solution(mesh):
    in_specs = (
        P("ao", None, None, "fit"),
        P(("fit", "ao"), None, None),
        P(),
        P("ao", "fit"),
        P(("fit", "ao"), None),
        P(("fit", "ao")),
    )
    out_specs = P(("fit", "ao"), None, None)
    return jax.shard_map(
        on_device, mesh=mesh, in_specs=in_specs, out_specs=out_specs, check_vma=False
    )
```

```python
import jax
import jax.numpy as jnp
from jax import lax
from jax.experimental import pallas as pl
from jax.experimental.pallas import tpu as pltpu
from jax.sharding import PartitionSpec as P

MESH = pl.DeviceIdType.MESH
F32, BF16 = jnp.float32, jnp.bfloat16
NF, NA, SIDE = 8, 16, 4
MUB, TILES, SLOTS, CAP = 4, 16, 16, 2
W = 128
ORB = 2 * W
PIECE = W // 4
CHUNKS = 2
ROWS = W // CHUNKS
BAND = 16
BANDS = W // BAND
UNITS = MUB * BANDS
WIDE = 64
DEEP = 32
I16 = jnp.int16
HEAD = 16
CODED = ROWS + HEAD
TOP = 32766.0
STEP = 16.0
NT = (((1,), (1,)), ((), ()))


def each(start, stop, body):
    def step(i, carry):
        body(i)
        return carry

    lax.fori_loop(start, stop, step, 0)


def whole_kernel(
    owner_ref, screen_ref, tile_owner_ref, tile_slot_ref, occ_ref, three_ref, out_ref,
    half, flat, acc, late, gram, own, first, piece, second, both, done, coeff,
    scales, slots, send, recv, sums_of, bsend, brecv, tab,
    load, s1, r1, s2, r2, s3, r3, sa, ra, sb, rb,
):
    fit, ao = lax.axis_index("fit"), lax.axis_index("ao")
    me = fit * NA + ao
    z, y = lax.div(ao, SIDE), lax.rem(ao, SIDE)

    def fit_peer(i):
        return lax.rem(fit + i, NF)

    def ao_peer(i):
        return lax.rem(z + lax.div(i, SIDE), SIDE) * SIDE + lax.rem(y + lax.rem(i, SIDE), SIDE)

    def fetch(u):
        j, b = lax.div(u, BANDS), lax.rem(u, BANDS)
        rows = pl.ds(pl.multiple_of(b * BAND, BAND), BAND)
        return pltpu.make_async_copy(three_ref.at[j, :, rows], half.at[1, j, :, rows], load.at[u])

    each(0, UNITS, lambda u: fetch(u).start())

    barrier = pltpu.get_barrier_semaphore()

    def greet_fit(i):
        pl.semaphore_signal(barrier, inc=1, device_id=(fit_peer(i), ao), device_id_type=MESH)

    def greet_ao(i):
        pl.semaphore_signal(barrier, inc=1, device_id=(fit, ao_peer(i)), device_id_type=MESH)

    each(1, NF, greet_fit)
    each(1, NA, greet_ao)

    occ = occ_ref[...].astype(F32)
    for which in range(2):
        keep = jnp.where(owner_ref[which] == me, 1.0, 0.0).astype(F32)
        own[pl.ds(which * 4, 4)] = (occ * keep).astype(BF16).reshape(4, PIECE, W)

    def look(owner):
        count = jnp.int32(0)
        tile = [jnp.int32(TILES), jnp.int32(TILES)]
        for t in range(TILES):
            hit = tile_owner_ref[t] == owner
            for r in range(CAP):
                tile[r] = jnp.where(jnp.logical_and(hit, count == r), t, tile[r])
            count = count + jnp.where(hit, 1, 0)
        for r in range(CAP):
            tab[owner * CAP + r] = tile[r]

    def turn(u):
        fetch(u).wait()
        j, b = lax.div(u, BANDS), lax.rem(u, BANDS)
        rows = pl.ds(pl.multiple_of(b * BAND, BAND), BAND)
        block = jnp.swapaxes(half[1, j, :, rows, :], 0, 1)
        block = jnp.stack([block[m].T for m in range(BAND)], 0)
        flat[j, :, rows, :] = jnp.swapaxes(block, 0, 1)

    def turn_and_look(u):
        turn(u)
        look(u - 12)

    each(0, 6, turn)
    pl.semaphore_wait(barrier, NF - 1 + NA - 1)

    def hop1(i):
        peer = fit_peer(i)
        return pltpu.make_async_remote_copy(
            src_ref=own.at[peer], dst_ref=first.at[i], send_sem=s1.at[i], recv_sem=r1.at[i],
            device_id=(peer, ao), device_id_type=MESH)

    def hop2(i):
        return pltpu.make_async_remote_copy(
            src_ref=piece, dst_ref=second.at[i], send_sem=s2.at[i], recv_sem=r2.at[i],
            device_id=(fit, ao_peer(i)), device_id_type=MESH)

    def hop3(i):
        return pltpu.make_async_remote_copy(
            src_ref=both, dst_ref=done.at[i], send_sem=s3.at[i], recv_sem=r3.at[i],
            device_id=(fit_peer(i), ao), device_id_type=MESH)

    def hop_a(c, i):
        return pltpu.make_async_remote_copy(
            src_ref=send.at[c, i], dst_ref=recv.at[c, i], send_sem=sa.at[c, i], recv_sem=ra.at[c, i],
            device_id=(fit, ao_peer(i)), device_id_type=MESH)

    def hop_b(c, i):
        peer = fit_peer(i)
        return pltpu.make_async_remote_copy(
            src_ref=bsend.at[c, peer], dst_ref=brecv.at[c, i], send_sem=sb.at[c, i], recv_sem=rb.at[c, i],
            device_id=(peer, ao), device_id_type=MESH)

    each(1, NF, lambda i: hop1(i).start())
    each(6, 12, turn)

    each(1, NF, lambda i: hop1(i).wait_recv())
    total = own[fit].astype(F32)
    for i in range(1, NF):
        total = total + first[i].astype(F32)
    piece[...] = total.astype(BF16)
    each(1, NA, lambda i: hop2(i).start())

    each(0, NA, look)
    each(12, 22, turn)
    each(1, NA, lambda i: hop2(i).wait_recv())
    for i in range(1, NA):
        total = total + second[i].astype(F32)
    both[...] = total.astype(BF16)
    each(1, NF, lambda i: hop3(i).start())
    coeff[fit] = both[...]
    each(22, 32, turn)
    each(1, NF, lambda i: hop3(i).wait_recv())

    def put(i):
        coeff[lax.rem(fit + NF - i, NF)] = done[i]

    each(1, NF, put)

    pair = coeff[...].reshape(2, W, W)
    orbitals = jnp.concatenate([pair[0], pair[1]], 1)

    def product(v):
        j = lax.div(v, W // WIDE)
        some = pl.ds(pl.multiple_of(lax.rem(v, W // WIDE) * WIDE, WIDE), WIDE)
        r = jnp.dot(flat[j, some].reshape(WIDE * W, W), orbitals, preferred_element_type=F32)
        r = r.astype(BF16)
        half[0, j, some] = r[:, :W].reshape(WIDE, W, W)
        half[1, j, some] = r[:, W:].reshape(WIDE, W, W)

    each(0, MUB * W // WIDE, product)

    def rows_of(first, lo, n):
        return jnp.concatenate(
            [half[h, :, first + v, lo:lo + n, :].reshape(MUB * n, W)
             for h in range(2) for v in range(DEEP)], 1)

    head_row = lax.broadcasted_iota(jnp.int32, (HEAD, W), 0)

    def encode(tile, slot):
        top = jnp.maximum(jnp.max(jnp.abs(tile), axis=0, keepdims=True), 1e-33)
        level = jnp.ceil(jnp.log2(top) * STEP)
        values = jnp.round(tile * (TOP * jnp.exp2(level * (-1.0 / STEP))))
        head = jnp.where(head_row == 0, level.astype(jnp.int32), slot)
        return values.astype(jnp.int32).astype(I16), head.astype(I16)

    def decode_head(head):
        head = head.astype(jnp.int32).astype(F32)
        return jnp.exp2(head[0:1] * (1.0 / STEP)) * (1.0 / TOP), head[1:2]

    def decode(values):
        return values.astype(jnp.int32).astype(F32)

    def fill(c, i, where_to):
        owner = ao_peer(i)
        for r in range(CAP):
            where_to[c, i, pl.ds(r * CODED, CODED)] = gram[c, tab[owner * CAP + r]]

    def early_tile(j, k):
        return acc[j * ROWS:(j + 1) * ROWS, k * W:(k + 1) * W]

    def late_tile(j, k):
        other = late[k * ROWS:(k + 1) * ROWS, j // 2 * W:(j // 2 + 1) * W]
        if j % 2 == 0:
            other = pltpu.roll(other, ROWS, 1)
        column = jnp.concatenate([acc[k * ROWS:(k + 1) * ROWS, j * W:(j + 1) * W], other], 0)
        return column.T[ROWS:]

    for c in range(CHUNKS):
        if c == 0:
            acc[...] = jnp.zeros_like(acc)

            def deep(i):
                acc[...] += lax.dot_general(
                    rows_of(i * DEEP, 0, ROWS), rows_of(i * DEEP, 0, W), NT,
                    preferred_element_type=F32)
        else:
            late[...] = jnp.zeros_like(late)

            def deep(i):
                side = rows_of(i * DEEP, ROWS, ROWS)
                late[...] += lax.dot_general(side, side, NT, preferred_element_type=F32)

        each(0, W // DEEP, deep)
        tile_at = late_tile if c else early_tile
        for j in range(MUB):
            for k in range(MUB):
                keep = (screen_ref[j] * screen_ref[k]).astype(F32)
                t = j * MUB + k
                values, head = encode(tile_at(j, k) * keep, tile_slot_ref[t])
                gram[c, t, pl.ds(0, ROWS)] = values
                gram[c, t, pl.ds(ROWS, HEAD)] = head
        gram[c, TILES] = jnp.full((CODED, W), -1, jnp.int32).astype(I16)

        def push(i, c=c):
            fill(c, i, send)
            hop_a(c, i).start()

        each(1, NA, push)
        fill(c, jnp.int32(0), recv)

    for c in range(CHUNKS):
        each(1, NA, lambda i, c=c: hop_a(c, i).wait_recv())

        def heads(i, c=c):
            for r in range(CAP):
                scale, slot = decode_head(recv[c, i, pl.ds(r * CODED + ROWS, HEAD)])
                scales[i, pl.ds(r * 8, 8)] = jnp.broadcast_to(scale, (8, W))
                slots[i, pl.ds(r * 8, 8)] = jnp.broadcast_to(slot, (8, W))

        each(0, NA, heads)

        def band(b, c=c):
            for group in range(0, SLOTS, 8):
                def add(i, sums, group=group):
                    for r in range(CAP):
                        tile = decode(recv[c, i, pl.ds(r * CODED + b * 16, 16)]).reshape(2, 8, W)
                        tile = tile * scales[i, pl.ds(r * 8, 8)][None]
                        slot = slots[i, pl.ds(r * 8, 8)]
                        sums = [
                            sums[q] + jnp.where((slot == float(group + q))[None], tile, 0.0)
                            for q in range(8)]
                    return sums

                zero = jnp.zeros((2, 8, W), F32)
                sums = lax.fori_loop(0, NA, add, [zero] * 8, unroll=4)
                for q in range(8):
                    sums_of[c, group + q, pl.ds(b * 16, 16)] = sums[q].reshape(16, W)

        each(0, ROWS // 16, band)

        def pack(q, c=c):
            values, head = encode(sums_of[c, q], jnp.int32(0))
            place = lax.rem(q, 2) * CODED
            bsend[c, lax.div(q, 2), pl.ds(pl.multiple_of(place, 16), ROWS)] = values
            bsend[c, lax.div(q, 2), pl.ds(pl.multiple_of(place + ROWS, 16), HEAD)] = head

        each(0, SLOTS, pack)
        each(1, NF, lambda i, c=c: hop_b(c, i).start())

    for c in range(CHUNKS):
        each(1, NF, lambda i, c=c: hop_b(c, i).wait_recv())
        for q in range(2):
            sums = sums_of[c, fit * 2 + q]
            for i in range(1, NF):
                scale, _ = decode_head(brecv[c, i, pl.ds(q * CODED + ROWS, HEAD)])
                sums = sums + decode(brecv[c, i, pl.ds(q * CODED, ROWS)]) * scale
            out_ref[q, pl.ds(c * ROWS, ROWS)] = sums

    each(1, NF, lambda i: hop1(i).wait_send())
    each(1, NA, lambda i: hop2(i).wait_send())
    each(1, NF, lambda i: hop3(i).wait_send())
    for c in range(CHUNKS):
        each(1, NA, lambda i, c=c: hop_a(c, i).wait_send())
        each(1, NF, lambda i, c=c: hop_b(c, i).wait_send())


def on_device(three_index, occ_coeff, occ_owner, screen, tile_owner, tile_slot):
    smem = pl.BlockSpec(memory_space=pltpu.SMEM)
    vmem = pl.BlockSpec(memory_space=pltpu.VMEM)
    dma = pltpu.SemaphoreType.DMA
    part = (PIECE, W)
    return pl.pallas_call(
        whole_kernel,
        out_shape=jax.ShapeDtypeStruct((2, W, W), F32),
        in_specs=[smem, smem, smem, smem, vmem, pl.BlockSpec(memory_space=pl.ANY)],
        out_specs=vmem,
        scratch_shapes=[
            pltpu.VMEM((2, MUB, W, W, W), BF16),
            pltpu.VMEM((MUB, W, W, W), BF16),
            pltpu.VMEM((MUB * ROWS, MUB * W), F32),
            pltpu.VMEM((MUB * ROWS, MUB * ROWS), F32),
            pltpu.VMEM((CHUNKS, TILES + 1, CODED, W), I16),
            pltpu.VMEM((NF,) + part, BF16),
            pltpu.VMEM((NF,) + part, BF16),
            pltpu.VMEM(part, BF16),
            pltpu.VMEM((NA,) + part, BF16),
            pltpu.VMEM(part, BF16),
            pltpu.VMEM((NF,) + part, BF16),
            pltpu.VMEM((NF,) + part, BF16),
            pltpu.VMEM((NA, CAP * 8, W), F32),
            pltpu.VMEM((NA, CAP * 8, W), F32),
            pltpu.VMEM((CHUNKS, NA, CAP * CODED, W), I16),
            pltpu.VMEM((CHUNKS, NA, CAP * CODED, W), I16),
            pltpu.VMEM((CHUNKS, SLOTS, ROWS, W), F32),
            pltpu.VMEM((CHUNKS, NF, 2 * CODED, W), I16),
            pltpu.VMEM((CHUNKS, NF, 2 * CODED, W), I16),
            pltpu.SMEM((NA * CAP,), jnp.int32),
            dma((UNITS,)),
            dma((NF,)), dma((NF,)), dma((NA,)), dma((NA,)), dma((NF,)), dma((NF,)),
            dma((CHUNKS, NA)), dma((CHUNKS, NA)), dma((CHUNKS, NF)), dma((CHUNKS, NF)),
        ],
        compiler_params=pltpu.CompilerParams(
            collective_id=0, has_side_effects=True, vmem_limit_bytes=63 << 20),
        name="exchange",
    )(occ_owner, screen[:, 0], tile_owner[:, 0], tile_slot, occ_coeff[0], three_index)


def solution(mesh):
    in_specs = (
        P("ao", None, None, "fit"),
        P(("fit", "ao"), None, None),
        P(),
        P("ao", "fit"),
        P(("fit", "ao"), None),
        P(("fit", "ao")),
    )
    out_specs = P(("fit", "ao"), None, None)
    return jax.shard_map(
        on_device, mesh=mesh, in_specs=in_specs, out_specs=out_specs, check_vma=False
    )
```

```python
import jax
import jax.numpy as jnp
from jax import lax
from jax.experimental import pallas as pl
from jax.experimental.pallas import tpu as pltpu
from jax.sharding import PartitionSpec as P

MESH = pl.DeviceIdType.MESH
F32, BF16 = jnp.float32, jnp.bfloat16
NF, NA, SIDE = 8, 16, 4
MUB, TILES, SLOTS, CAP = 4, 16, 16, 2
W = 128
ORB = 2 * W
PIECE = W // 4
PARTS = 4
ROWS = W // 2
BAND = 16
BANDS = W // BAND
UNITS = MUB * BANDS
WIDE = 128
DEEP = 32
I16 = jnp.int16
HEAD = 16
CODED = ROWS + HEAD
TOP = 32766.0
STEP = 16.0
NT = (((1,), (1,)), ((), ()))


def every(start, stop, body):
    for i in range(start, stop):
        body(i)


def each(start, stop, body):
    def step(i, carry):
        body(i)
        return carry

    lax.fori_loop(start, stop, step, 0)


def whole_kernel(
    owner_ref, screen_ref, tile_owner_ref, tile_slot_ref, occ_ref, three_ref, out_ref,
    half, flat, acc, gram, own, first, piece, second, both, done, coeff,
    scales, slots, send, recv, sums_of, mine, bsend, brecv, tab,
    load, s1, r1, s2, r2, s3, r3, sa, ra, sb, rb,
):
    fit, ao = lax.axis_index("fit"), lax.axis_index("ao")
    me = fit * NA + ao
    z, y = lax.div(ao, SIDE), lax.rem(ao, SIDE)

    def fit_peer(i):
        return lax.rem(fit + i, NF)

    def ao_peer(i):
        dz, dy = (i // SIDE, i % SIDE) if isinstance(i, int) else (lax.div(i, SIDE), lax.rem(i, SIDE))
        return lax.rem(z + dz, SIDE) * SIDE + lax.rem(y + dy, SIDE)

    def fetch(u):
        j, b = lax.div(u, BANDS), lax.rem(u, BANDS)
        rows = pl.ds(pl.multiple_of(b * BAND, BAND), BAND)
        return pltpu.make_async_copy(three_ref.at[j, :, rows], half.at[1, j, :, rows], load.at[u])

    each(0, UNITS, lambda u: fetch(u).start())

    barrier = pltpu.get_barrier_semaphore()

    def greet_fit(i):
        pl.semaphore_signal(barrier, inc=1, device_id=(fit_peer(i), ao), device_id_type=MESH)

    def greet_ao(i):
        pl.semaphore_signal(barrier, inc=1, device_id=(fit, ao_peer(i)), device_id_type=MESH)

    every(1, NF, greet_fit)
    every(1, NA, greet_ao)

    occ = occ_ref[...].astype(F32)
    for which in range(2):
        keep = jnp.where(owner_ref[which] == me, 1.0, 0.0).astype(F32)
        own[pl.ds(which * 4, 4)] = (occ * keep).astype(BF16).reshape(4, PIECE, W)

    def look(owner):
        count = jnp.int32(0)
        tile = [jnp.int32(TILES), jnp.int32(TILES)]
        for t in range(TILES):
            hit = tile_owner_ref[t] == owner
            for r in range(CAP):
                tile[r] = jnp.where(jnp.logical_and(hit, count == r), t, tile[r])
            count = count + jnp.where(hit, 1, 0)
        for r in range(CAP):
            tab[owner * CAP + r] = tile[r]

    def turn(u):
        fetch(u).wait()
        j, b = lax.div(u, BANDS), lax.rem(u, BANDS)
        rows = pl.ds(pl.multiple_of(b * BAND, BAND), BAND)
        block = jnp.swapaxes(half[1, j, :, rows, :], 0, 1)
        block = jnp.stack([block[m].T for m in range(BAND)], 0)
        flat[j, :, rows, :] = jnp.swapaxes(block, 0, 1)

    def turn_and_look(u):
        turn(u)
        look(u - 12)

    each(0, 6, turn)
    pl.semaphore_wait(barrier, NF - 1 + NA - 1)

    def hop1(i):
        peer = fit_peer(i)
        return pltpu.make_async_remote_copy(
            src_ref=own.at[peer], dst_ref=first.at[i], send_sem=s1.at[i], recv_sem=r1.at[i],
            device_id=(peer, ao), device_id_type=MESH)

    def hop2(i):
        return pltpu.make_async_remote_copy(
            src_ref=piece, dst_ref=second.at[i], send_sem=s2.at[i], recv_sem=r2.at[i],
            device_id=(fit, ao_peer(i)), device_id_type=MESH)

    def hop3(i):
        return pltpu.make_async_remote_copy(
            src_ref=both, dst_ref=done.at[i], send_sem=s3.at[i], recv_sem=r3.at[i],
            device_id=(fit_peer(i), ao), device_id_type=MESH)

    def hop_a(c, i):
        return pltpu.make_async_remote_copy(
            src_ref=send.at[c, i], dst_ref=recv.at[c, i], send_sem=sa.at[c, i], recv_sem=ra.at[c, i],
            device_id=(fit, ao_peer(i)), device_id_type=MESH)

    def hop_b(c, i):
        peer = fit_peer(i)
        return pltpu.make_async_remote_copy(
            src_ref=bsend.at[c, peer], dst_ref=brecv.at[c, i], send_sem=sb.at[c, i], recv_sem=rb.at[c, i],
            device_id=(peer, ao), device_id_type=MESH)

    every(1, NF, lambda i: hop1(i).start())
    each(6, 12, turn)

    every(1, NF, lambda i: hop1(i).wait_recv())
    total = own[fit].astype(F32)
    for i in range(1, NF):
        total = total + first[i].astype(F32)
    piece[...] = total.astype(BF16)
    every(1, NA, lambda i: hop2(i).start())

    each(0, NA, look)
    each(12, 22, turn)
    every(1, NA, lambda i: hop2(i).wait_recv())
    for i in range(1, NA):
        total = total + second[i].astype(F32)
    both[...] = total.astype(BF16)
    every(1, NF, lambda i: hop3(i).start())
    coeff[fit] = both[...]
    each(22, 32, turn)
    every(1, NF, lambda i: hop3(i).wait_recv())

    def put(i):
        coeff[lax.rem(fit + NF - i, NF)] = done[i]

    each(1, NF, put)

    pair = coeff[...].reshape(2, W, W)
    orbitals = jnp.concatenate([pair[0], pair[1]], 1)

    def product(v):
        j = lax.div(v, W // WIDE)
        some = pl.ds(pl.multiple_of(lax.rem(v, W // WIDE) * WIDE, WIDE), WIDE)
        r = jnp.dot(flat[j, some].reshape(WIDE * W, W), orbitals, preferred_element_type=F32)
        r = r.astype(BF16)
        half[0, j, some] = r[:, :W].reshape(WIDE, W, W)
        half[1, j, some] = r[:, W:].reshape(WIDE, W, W)

    each(0, MUB * W // WIDE, product)

    def rows_of(first, lo, n):
        return jnp.concatenate(
            [half[h, :, first + v, lo:lo + n, :].reshape(MUB * n, W)
             for h in range(2) for v in range(DEEP)], 1)

    head_row = lax.broadcasted_iota(jnp.int32, (HEAD, W), 0)

    def encode(tile, slot):
        top = jnp.maximum(jnp.max(jnp.abs(tile), axis=0, keepdims=True), 1e-33)
        level = jnp.ceil(jnp.log2(top) * STEP)
        values = jnp.round(tile * (TOP * jnp.exp2(level * (-1.0 / STEP))))
        head = jnp.where(head_row == 0, level.astype(jnp.int32), slot)
        return values.astype(jnp.int32).astype(I16), head.astype(I16)

    def decode_head(head):
        head = head.astype(jnp.int32).astype(F32)
        return jnp.exp2(head[0:1] * (1.0 / STEP)) * (1.0 / TOP), head[1:2]

    def decode(values):
        return values.astype(jnp.int32).astype(F32)

    left = lax.broadcasted_iota(jnp.int32, (CODED, W), 1) < ROWS
    left_row = left[:ROWS]

    def fill(p, i, where_to):
        owner = ao_peer(i)
        one = gram[p, tab[owner * CAP]].astype(jnp.int32)
        two = gram[p, tab[owner * CAP + 1]].astype(jnp.int32)
        where_to[p, i] = jnp.where(left, one, two).astype(I16)

    def store(p, t, tile):
        keep = (screen_ref[t // MUB] * screen_ref[t % MUB]).astype(F32)
        values, head = encode(tile * keep, tile_slot_ref[t])
        gram[p, t, pl.ds(0, ROWS)] = values
        gram[p, t, pl.ds(ROWS, HEAD)] = head

    def share(p):
        gram[p, TILES] = jnp.full((CODED, W), -1, jnp.int32).astype(I16)

        def push(i):
            fill(p, i, send)
            hop_a(p, i).start()

        each(1, NA, push)
        fill(p, 0, recv)

    def block(stage, j, k):
        return acc[stage, j * ROWS:(j + 1) * ROWS, k // 2 * W:(k // 2 + 1) * W]

    for stage, (a, b) in enumerate(((0, 0), (0, 1), (1, 1))):
        acc[stage] = jnp.zeros((MUB * ROWS, MUB * ROWS), F32)

        def deep(i, stage=stage, a=a, b=b):
            one = rows_of(i * DEEP, a * ROWS, ROWS)
            two = one if a == b else rows_of(i * DEEP, b * ROWS, ROWS)
            acc[stage] += lax.dot_general(one, two, NT, preferred_element_type=F32)

        each(0, W // DEEP, deep)
        for j in range(MUB):
            for k in range(MUB):
                tile = block(stage, j, k)
                other = pltpu.roll(tile, ROWS, 1)
                pair = (tile, other) if k % 2 == 0 else (other, tile)
                store(a * 2 + b, j * MUB + k, jnp.where(left_row, pair[0], pair[1]))
        share(a * 2 + b)
        if a != b:
            for k in range(MUB):
                for j in range(0, MUB, 2):
                    tile = block(stage, k, j)
                    turned = jnp.concatenate([tile, tile], 0).T
                    store(2, j * MUB + k, turned[:ROWS])
                    store(2, (j + 1) * MUB + k, turned[ROWS:])
            share(2)

    order = (0, 1, 2, 3)
    for p in order:
        each(1, NA, lambda i, p=p: hop_a(p, i).wait_recv())

        def heads(i, p=p):
            scale, slot = decode_head(recv[p, i, pl.ds(ROWS, HEAD)])
            scales[i] = jnp.broadcast_to(scale, (8, W))
            slots[i] = jnp.broadcast_to(slot, (8, W))

        each(0, NA, heads)

        def band(b, p=p):
            for group in range(0, SLOTS, 8):
                def add(i, sums, group=group):
                    tile = decode(recv[p, i, pl.ds(b * 16, 16)]).reshape(2, 8, W) * scales[i][None]
                    slot = slots[i]
                    return [
                        sums[q] + jnp.where((slot == float(group + q))[None], tile, 0.0)
                        for q in range(8)]

                zero = jnp.zeros((2, 8, W), F32)
                sums = lax.fori_loop(0, NA, add, [zero] * 8, unroll=4)
                for q in range(0, 8, 2):
                    even, odd = sums[q].reshape(16, W), sums[q + 1].reshape(16, W)
                    swapped = pltpu.roll(jnp.where(left[:16], odd, even), ROWS, 1)
                    sums_of[(group + q) // 2, pl.ds(b * 16, 16)] = jnp.where(left[:16], even, odd) + swapped

        each(0, ROWS // 16, band)

        def pack(g, p=p):
            values, head = encode(sums_of[g], jnp.int32(0))
            bsend[p, g, pl.ds(0, ROWS)] = values
            bsend[p, g, pl.ds(ROWS, HEAD)] = head

        each(0, NF, pack)
        each(1, NF, lambda i, p=p: hop_b(p, i).start())
        mine[p] = sums_of[fit]

    every(1, NF, lambda i: hop1(i).wait_send())
    every(1, NA, lambda i: hop2(i).wait_send())
    every(1, NF, lambda i: hop3(i).wait_send())
    for p in order:
        each(1, NA, lambda i, p=p: hop_a(p, i).wait_send())

    def fit_sum(p):
        each(1, NF, lambda i: hop_b(p, i).wait_recv())
        sums = mine[p]
        for i in range(1, NF):
            scale, _ = decode_head(brecv[p, i, pl.ds(ROWS, HEAD)])
            sums = sums + decode(brecv[p, i, pl.ds(0, ROWS)]) * scale
        return sums

    for a in range(2):
        one, two = fit_sum(2 * a), fit_sum(2 * a + 1)
        rows = pl.ds(a * ROWS, ROWS)
        out_ref[0, rows] = jnp.where(left_row, one, pltpu.roll(two, ROWS, 1))
        out_ref[1, rows] = jnp.where(left_row, pltpu.roll(one, ROWS, 1), two)

    for p in order:
        each(1, NF, lambda i, p=p: hop_b(p, i).wait_send())


def on_device(three_index, occ_coeff, occ_owner, screen, tile_owner, tile_slot):
    smem = pl.BlockSpec(memory_space=pltpu.SMEM)
    vmem = pl.BlockSpec(memory_space=pltpu.VMEM)
    dma = pltpu.SemaphoreType.DMA
    part = (PIECE, W)
    return pl.pallas_call(
        whole_kernel,
        out_shape=jax.ShapeDtypeStruct((2, W, W), F32),
        in_specs=[smem, smem, smem, smem, vmem, pl.BlockSpec(memory_space=pl.ANY)],
        out_specs=vmem,
        scratch_shapes=[
            pltpu.VMEM((2, MUB, W, W, W), BF16),
            pltpu.VMEM((MUB, W, W, W), BF16),
            pltpu.VMEM((3, MUB * ROWS, MUB * ROWS), F32),
            pltpu.VMEM((PARTS, TILES + 1, CODED, W), I16),
            pltpu.VMEM((NF,) + part, BF16),
            pltpu.VMEM((NF,) + part, BF16),
            pltpu.VMEM(part, BF16),
            pltpu.VMEM((NA,) + part, BF16),
            pltpu.VMEM(part, BF16),
            pltpu.VMEM((NF,) + part, BF16),
            pltpu.VMEM((NF,) + part, BF16),
            pltpu.VMEM((NA, 8, W), F32),
            pltpu.VMEM((NA, 8, W), F32),
            pltpu.VMEM((PARTS, NA, CODED, W), I16),
            pltpu.VMEM((PARTS, NA, CODED, W), I16),
            pltpu.VMEM((NF, ROWS, W), F32),
            pltpu.VMEM((PARTS, ROWS, W), F32),
            pltpu.VMEM((PARTS, NF, CODED, W), I16),
            pltpu.VMEM((PARTS, NF, CODED, W), I16),
            pltpu.SMEM((NA * CAP,), jnp.int32),
            dma((UNITS,)),
            dma((NF,)), dma((NF,)), dma((NA,)), dma((NA,)), dma((NF,)), dma((NF,)),
            dma((PARTS, NA)), dma((PARTS, NA)), dma((PARTS, NF)), dma((PARTS, NF)),
        ],
        compiler_params=pltpu.CompilerParams(
            collective_id=0, has_side_effects=True, vmem_limit_bytes=63 << 20),
        name="exchange",
    )(occ_owner, screen[:, 0], tile_owner[:, 0], tile_slot, occ_coeff[0], three_index)


def solution(mesh):
    in_specs = (
        P("ao", None, None, "fit"),
        P(("fit", "ao"), None, None),
        P(),
        P("ao", "fit"),
        P(("fit", "ao"), None),
        P(("fit", "ao")),
    )
    out_specs = P(("fit", "ao"), None, None)
    return jax.shard_map(
        on_device, mesh=mesh, in_specs=in_specs, out_specs=out_specs, check_vma=False
    )
```

```python
import jax
import jax.numpy as jnp
from jax import lax
from jax.experimental import pallas as pl
from jax.experimental.pallas import tpu as pltpu
from jax.sharding import PartitionSpec as P

MESH = pl.DeviceIdType.MESH
F32, BF16 = jnp.float32, jnp.bfloat16
NF, NA, SIDE = 8, 16, 4
MUB, TILES, SLOTS, CAP = 4, 16, 16, 2
W = 128
ORB = 2 * W
PIECE = W // 4
PARTS = 4
ROWS = W // 2
BAND = 16
BANDS = W // BAND
UNITS = MUB * BANDS
WIDE = 128
DEEP = 64
I16 = jnp.int16
HEAD = 8
CODED = ROWS + HEAD
TOP = 32766.0
STEP = 16.0
NT = (((1,), (1,)), ((), ()))


def every(start, stop, body):
    for i in range(start, stop):
        body(i)


def each(start, stop, body):
    def step(i, carry):
        body(i)
        return carry

    lax.fori_loop(start, stop, step, 0)


def whole_kernel(
    owner_in, screen_in, tile_owner_in, tile_slot_in, occ_in, three_ref, out_hbm,
    out_ref, owner_ref, screen_ref, tile_owner_ref, tile_slot_ref, occ_ref,
    half, flat, acc, gram, own, first, piece, second, both, done, coeff,
    scales, slots, send, recv, sums_of, mine, sides, bsend, brecv, tab,
    load, small, s1, r1, s2, r2, s3, r3, sa, ra, sb, rb,
):
    fit, ao = lax.axis_index("fit"), lax.axis_index("ao")
    me = fit * NA + ao
    z, y = lax.div(ao, SIDE), lax.rem(ao, SIDE)

    def fit_peer(i):
        return lax.rem(fit + i, NF)

    def ao_peer(i):
        dz, dy = (i // SIDE, i % SIDE) if isinstance(i, int) else (lax.div(i, SIDE), lax.rem(i, SIDE))
        return lax.rem(z + dz, SIDE) * SIDE + lax.rem(y + dy, SIDE)

    def fetch(u):
        j, b = lax.div(u, BANDS), lax.rem(u, BANDS)
        rows = pl.ds(pl.multiple_of(b * BAND, BAND), BAND)
        return pltpu.make_async_copy(three_ref.at[j, :, rows], half.at[1, j, :, rows], load.at[u])

    smalls = [
        pltpu.make_async_copy(here, there, small.at[n])
        for n, (here, there) in enumerate((
            (owner_in, owner_ref), (occ_in, occ_ref), (tile_owner_in, tile_owner_ref),
            (tile_slot_in, tile_slot_ref), (screen_in, screen_ref)))]
    for copy in smalls:
        copy.start()
    each(0, UNITS, lambda u: fetch(u).start())

    barrier = pltpu.get_barrier_semaphore()

    def greet_fit(i):
        pl.semaphore_signal(barrier, inc=1, device_id=(fit_peer(i), ao), device_id_type=MESH)

    def greet_ao(i):
        pl.semaphore_signal(barrier, inc=1, device_id=(fit, ao_peer(i)), device_id_type=MESH)

    every(1, NF, greet_fit)
    every(1, NA, greet_ao)

    for copy in smalls:
        copy.wait()
    occ = occ_ref[...].astype(F32)
    for which in range(2):
        keep = jnp.where(owner_ref[which] == me, 1.0, 0.0).astype(F32)
        own[pl.ds(which * 4, 4)] = (occ * keep).astype(BF16).reshape(4, PIECE, W)

    def look(owner):
        count = jnp.int32(0)
        tile = [jnp.int32(TILES), jnp.int32(TILES)]
        for t in range(TILES):
            hit = tile_owner_ref[t] == owner
            for r in range(CAP):
                tile[r] = jnp.where(jnp.logical_and(hit, count == r), t, tile[r])
            count = count + jnp.where(hit, 1, 0)
        for r in range(CAP):
            tab[owner * CAP + r] = tile[r]

    def turn(u):
        fetch(u).wait()
        j, b = lax.div(u, BANDS), lax.rem(u, BANDS)
        rows = pl.ds(pl.multiple_of(b * BAND, BAND), BAND)
        block = jnp.swapaxes(half[1, j, :, rows, :], 0, 1)
        block = jnp.stack([block[m].T for m in range(BAND)], 0)
        flat[j, :, rows, :] = jnp.swapaxes(block, 0, 1)

    def turn_and_look(u):
        turn(u)
        look(u - 12)

    each(0, 6, turn)
    pl.semaphore_wait(barrier, NF - 1 + NA - 1)

    def hop1(i):
        peer = fit_peer(i)
        return pltpu.make_async_remote_copy(
            src_ref=own.at[peer], dst_ref=first.at[i], send_sem=s1.at[i], recv_sem=r1.at[i],
            device_id=(peer, ao), device_id_type=MESH)

    def hop2(i):
        return pltpu.make_async_remote_copy(
            src_ref=piece, dst_ref=second.at[i], send_sem=s2.at[i], recv_sem=r2.at[i],
            device_id=(fit, ao_peer(i)), device_id_type=MESH)

    def hop3(i):
        return pltpu.make_async_remote_copy(
            src_ref=both, dst_ref=done.at[i], send_sem=s3.at[i], recv_sem=r3.at[i],
            device_id=(fit_peer(i), ao), device_id_type=MESH)

    def hop_a(c, i):
        return pltpu.make_async_remote_copy(
            src_ref=send.at[c, i], dst_ref=recv.at[c, i], send_sem=sa.at[c, i], recv_sem=ra.at[c, i],
            device_id=(fit, ao_peer(i)), device_id_type=MESH)

    def hop_b(c, i):
        peer = fit_peer(i)
        return pltpu.make_async_remote_copy(
            src_ref=bsend.at[c, peer], dst_ref=brecv.at[c, i], send_sem=sb.at[c, i], recv_sem=rb.at[c, i],
            device_id=(peer, ao), device_id_type=MESH)

    every(1, NF, lambda i: hop1(i).start())
    each(6, 12, turn)

    every(1, NF, lambda i: hop1(i).wait_recv())
    total = own[fit].astype(F32)
    for i in range(1, NF):
        total = total + first[i].astype(F32)
    piece[...] = total.astype(BF16)
    every(1, NA, lambda i: hop2(i).start())

    each(0, NA, look)
    each(12, 22, turn)
    every(1, NA, lambda i: hop2(i).wait_recv())
    for i in range(1, NA):
        total = total + second[i].astype(F32)
    both[...] = total.astype(BF16)
    every(1, NF, lambda i: hop3(i).start())
    coeff[fit] = both[...]
    each(22, 32, turn)
    every(1, NF, lambda i: hop3(i).wait_recv())

    def put(i):
        coeff[lax.rem(fit + NF - i, NF)] = done[i]

    each(1, NF, put)

    pair = coeff[...].reshape(2, W, W)
    orbitals = jnp.concatenate([pair[0], pair[1]], 1)

    def product(v):
        j = lax.div(v, W // WIDE)
        some = pl.ds(pl.multiple_of(lax.rem(v, W // WIDE) * WIDE, WIDE), WIDE)
        r = jnp.dot(flat[j, some].reshape(WIDE * W, W), orbitals, preferred_element_type=F32)
        r = r.astype(BF16)
        half[0, j, some] = r[:, :W].reshape(WIDE, W, W)
        half[1, j, some] = r[:, W:].reshape(WIDE, W, W)

    each(0, MUB * W // WIDE, product)

    def rows_of(first, lo, n):
        return jnp.concatenate(
            [half[h, :, first + v, lo:lo + n, :].reshape(MUB * n, W)
             for h in range(2) for v in range(DEEP)], 1)

    head_row = lax.broadcasted_iota(jnp.int32, (HEAD, W), 0)

    def encode(tile, slot):
        top = jnp.maximum(jnp.max(jnp.abs(tile), axis=0, keepdims=True), 1e-33)
        level = jnp.ceil(jnp.log2(top) * STEP)
        values = jnp.round(tile * (TOP * jnp.exp2(level * (-1.0 / STEP))))
        head = jnp.where(head_row == 0, level.astype(jnp.int32), slot)
        return values.astype(jnp.int32).astype(I16), head.astype(I16)

    def decode_head(head):
        head = head.astype(jnp.int32).astype(F32)
        return jnp.exp2(head[0:1] * (1.0 / STEP)) * (1.0 / TOP), head[1:2]

    def decode(values):
        return values.astype(jnp.int32).astype(F32)

    left = lax.broadcasted_iota(jnp.int32, (CODED, W), 1) < ROWS
    left_row = left[:ROWS]
    sides[0] = jnp.where(left, -1, 0).astype(I16)
    sides[1] = jnp.where(left, 0, -1).astype(I16)

    def fill(p, i, where_to):
        owner = ao_peer(i)
        one, two = gram[p, tab[owner * CAP]], gram[p, tab[owner * CAP + 1]]
        where_to[p, i] = (one & sides[0]) | (two & sides[1])

    def store(p, t, tile):
        keep = (screen_ref[t // MUB] * screen_ref[t % MUB]).astype(F32)
        values, head = encode(tile * keep, tile_slot_ref[t])
        gram[p, t, pl.ds(0, ROWS)] = values
        gram[p, t, pl.ds(ROWS, HEAD)] = head

    def share(p):
        gram[p, TILES] = jnp.full((CODED, W), -1, jnp.int32).astype(I16)

        def push(i):
            fill(p, i, send)
            hop_a(p, i).start()

        each(1, NA, push)
        fill(p, 0, recv)

    def block(stage, j, k):
        return acc[stage, j * ROWS:(j + 1) * ROWS, k // 2 * W:(k // 2 + 1) * W]

    for stage, (a, b) in enumerate(((0, 0), (0, 1), (1, 1))):
        acc[stage] = jnp.zeros((MUB * ROWS, MUB * ROWS), F32)

        def deep(i, stage=stage, a=a, b=b):
            one = rows_of(i * DEEP, a * ROWS, ROWS)
            two = one if a == b else rows_of(i * DEEP, b * ROWS, ROWS)
            acc[stage] += lax.dot_general(one, two, NT, preferred_element_type=F32)

        each(0, W // DEEP, deep)
        for j in range(MUB):
            for k in range(MUB):
                tile = block(stage, j, k)
                other = pltpu.roll(tile, ROWS, 1)
                pair = (tile, other) if k % 2 == 0 else (other, tile)
                store(a * 2 + b, j * MUB + k, jnp.where(left_row, pair[0], pair[1]))
        share(a * 2 + b)
        if a != b:
            for k in range(MUB):
                for j in range(0, MUB, 2):
                    tile = block(stage, k, j)
                    turned = jnp.concatenate([tile, tile], 0).T
                    store(2, j * MUB + k, turned[:ROWS])
                    store(2, (j + 1) * MUB + k, turned[ROWS:])
            share(2)

    order = (0, 1, 2, 3)
    for p in order:
        each(1, NA, lambda i, p=p: hop_a(p, i).wait_recv())

        def heads(i, p=p):
            scale, slot = decode_head(recv[p, i, pl.ds(ROWS, HEAD)])
            scales[i] = jnp.broadcast_to(scale, (8, W))
            slots[i] = jnp.broadcast_to(slot, (8, W))

        each(0, NA, heads)

        def band(b, p=p):
            for group in range(0, SLOTS, 8):
                def add(i, sums, group=group):
                    tile = decode(recv[p, i, pl.ds(b * 16, 16)]).reshape(2, 8, W) * scales[i][None]
                    slot = slots[i]
                    return [
                        sums[q] + jnp.where((slot == float(group + q))[None], tile, 0.0)
                        for q in range(8)]

                zero = jnp.zeros((2, 8, W), F32)
                sums = lax.fori_loop(0, NA, add, [zero] * 8, unroll=16)
                for q in range(0, 8, 2):
                    even, odd = sums[q].reshape(16, W), sums[q + 1].reshape(16, W)
                    swapped = pltpu.roll(jnp.where(left[:16], odd, even), ROWS, 1)
                    sums_of[(group + q) // 2, pl.ds(b * 16, 16)] = jnp.where(left[:16], even, odd) + swapped

        each(0, ROWS // 16, band)

        def pack(g, p=p):
            values, head = encode(sums_of[g], jnp.int32(0))
            bsend[p, g, pl.ds(0, ROWS)] = values
            bsend[p, g, pl.ds(ROWS, HEAD)] = head

        each(0, NF, pack)
        each(1, NF, lambda i, p=p: hop_b(p, i).start())
        mine[p] = sums_of[fit]

    every(1, NF, lambda i: hop1(i).wait_send())
    every(1, NA, lambda i: hop2(i).wait_send())
    every(1, NF, lambda i: hop3(i).wait_send())
    for p in order:
        each(1, NA, lambda i, p=p: hop_a(p, i).wait_send())

    def fit_sum(p):
        each(1, NF, lambda i: hop_b(p, i).wait_recv())
        sums = mine[p]
        for i in range(1, NF):
            scale, _ = decode_head(brecv[p, i, pl.ds(ROWS, HEAD)])
            sums = sums + decode(brecv[p, i, pl.ds(0, ROWS)]) * scale
        return sums

    def leave(a):
        rows = pl.ds(a * ROWS, ROWS)
        return pltpu.make_async_copy(out_ref.at[:, rows], out_hbm.at[:, rows], small.at[a])

    for a in range(2):
        one, two = fit_sum(2 * a), fit_sum(2 * a + 1)
        rows = pl.ds(a * ROWS, ROWS)
        out_ref[0, rows] = jnp.where(left_row, one, pltpu.roll(two, ROWS, 1))
        out_ref[1, rows] = jnp.where(left_row, pltpu.roll(one, ROWS, 1), two)
        leave(a).start()

    for p in order:
        each(1, NF, lambda i, p=p: hop_b(p, i).wait_send())
    for a in range(2):
        leave(a).wait()


def on_device(three_index, occ_coeff, occ_owner, screen, tile_owner, tile_slot):
    dma = pltpu.SemaphoreType.DMA
    part = (PIECE, W)
    return pl.pallas_call(
        whole_kernel,
        out_shape=jax.ShapeDtypeStruct((2, W, W), F32),
        in_specs=[pl.BlockSpec(memory_space=pl.ANY)] * 6,
        out_specs=pl.BlockSpec(memory_space=pl.ANY),
        scratch_shapes=[
            pltpu.VMEM((2, W, W), F32),
            pltpu.SMEM((2,), jnp.int32),
            pltpu.SMEM((MUB,), jnp.int32),
            pltpu.SMEM((TILES,), jnp.int32),
            pltpu.SMEM((TILES,), jnp.int32),
            pltpu.VMEM((W, W), BF16),
            pltpu.VMEM((2, MUB, W, W, W), BF16),
            pltpu.VMEM((MUB, W, W, W), BF16),
            pltpu.VMEM((3, MUB * ROWS, MUB * ROWS), F32),
            pltpu.VMEM((PARTS, TILES + 1, CODED, W), I16),
            pltpu.VMEM((NF,) + part, BF16),
            pltpu.VMEM((NF,) + part, BF16),
            pltpu.VMEM(part, BF16),
            pltpu.VMEM((NA,) + part, BF16),
            pltpu.VMEM(part, BF16),
            pltpu.VMEM((NF,) + part, BF16),
            pltpu.VMEM((NF,) + part, BF16),
            pltpu.VMEM((NA, 8, W), F32),
            pltpu.VMEM((NA, 8, W), F32),
            pltpu.VMEM((PARTS, NA, CODED, W), I16),
            pltpu.VMEM((PARTS, NA, CODED, W), I16),
            pltpu.VMEM((NF, ROWS, W), F32),
            pltpu.VMEM((PARTS, ROWS, W), F32),
            pltpu.VMEM((2, CODED, W), I16),
            pltpu.VMEM((PARTS, NF, CODED, W), I16),
            pltpu.VMEM((PARTS, NF, CODED, W), I16),
            pltpu.SMEM((NA * CAP,), jnp.int32),
            dma((UNITS,)), dma((5,)),
            dma((NF,)), dma((NF,)), dma((NA,)), dma((NA,)), dma((NF,)), dma((NF,)),
            dma((PARTS, NA)), dma((PARTS, NA)), dma((PARTS, NF)), dma((PARTS, NF)),
        ],
        compiler_params=pltpu.CompilerParams(
            collective_id=0, has_side_effects=True, vmem_limit_bytes=63 << 20),
        name="exchange",
    )(occ_owner, screen[:, 0], tile_owner[:, 0], tile_slot, occ_coeff[0], three_index)


def solution(mesh):
    in_specs = (
        P("ao", None, None, "fit"),
        P(("fit", "ao"), None, None),
        P(),
        P("ao", "fit"),
        P(("fit", "ao"), None),
        P(("fit", "ao")),
    )
    out_specs = P(("fit", "ao"), None, None)
    return jax.shard_map(
        on_device, mesh=mesh, in_specs=in_specs, out_specs=out_specs, check_vma=False
    )
```

```python
import jax
import jax.numpy as jnp
from jax import lax
from jax.experimental import pallas as pl
from jax.experimental.pallas import tpu as pltpu
from jax.sharding import PartitionSpec as P

MESH = pl.DeviceIdType.MESH
F32, BF16 = jnp.float32, jnp.bfloat16
NF, NA, SIDE = 8, 16, 4
MUB, TILES, SLOTS, CAP = 4, 16, 16, 2
W = 128
ORB = 2 * W
PIECE = W // 4
PARTS = 4
ROWS = W // 2
BAND = 16
BANDS = W // BAND
UNITS = MUB * BANDS
WIDE = 128
DEEP = 64
I16 = jnp.int16
HEAD = 8
CODED = ROWS + HEAD
TOP = 32766.0
STEP = 16.0
NT = (((1,), (1,)), ((), ()))


def every(start, stop, body):
    for i in range(start, stop):
        body(i)


def each(start, stop, body):
    def step(i, carry):
        body(i)
        return carry

    lax.fori_loop(start, stop, step, 0)


def whole_kernel(
    owner_in, screen_in, tile_owner_in, tile_slot_in, occ_in, three_ref, out_hbm,
    out_ref, owner_ref, screen_ref, tile_owner_ref, tile_slot_ref, occ_ref,
    half, flat, acc, gram, own, first, piece, second, both, done, coeff,
    scales, slots, send, recv, sums_of, mine, sides, bsend, brecv, tab,
    load, small, s1, r1, s2, r2, s3, r3, sa, ra, sb, rb,
):
    fit, ao = lax.axis_index("fit"), lax.axis_index("ao")
    me = fit * NA + ao
    z, y = lax.div(ao, SIDE), lax.rem(ao, SIDE)

    def fit_peer(i):
        return lax.rem(fit + i, NF)

    def ao_peer(i):
        dz, dy = (i // SIDE, i % SIDE) if isinstance(i, int) else (lax.div(i, SIDE), lax.rem(i, SIDE))
        return lax.rem(z + dz, SIDE) * SIDE + lax.rem(y + dy, SIDE)

    def fetch(u):
        j, b = lax.div(u, BANDS), lax.rem(u, BANDS)
        rows = pl.ds(pl.multiple_of(b * BAND, BAND), BAND)
        return pltpu.make_async_copy(three_ref.at[j, :, rows], half.at[1, j, :, rows], load.at[u])

    smalls = [
        pltpu.make_async_copy(here, there, small.at[n])
        for n, (here, there) in enumerate((
            (owner_in, owner_ref), (occ_in, occ_ref), (tile_owner_in, tile_owner_ref),
            (tile_slot_in, tile_slot_ref), (screen_in, screen_ref)))]
    for copy in smalls:
        copy.start()
    each(0, UNITS, lambda u: fetch(u).start())

    barrier = pltpu.get_barrier_semaphore()

    def greet_fit(i):
        pl.semaphore_signal(barrier, inc=1, device_id=(fit_peer(i), ao), device_id_type=MESH)

    def greet_ao(i):
        pl.semaphore_signal(barrier, inc=1, device_id=(fit, ao_peer(i)), device_id_type=MESH)

    every(1, NF, greet_fit)
    every(1, NA, greet_ao)

    for copy in smalls:
        copy.wait()
    occ = occ_ref[...].astype(F32)
    for which in range(2):
        keep = jnp.where(owner_ref[which] == me, 1.0, 0.0).astype(F32)
        own[pl.ds(which * 4, 4)] = (occ * keep).astype(BF16).reshape(4, PIECE, W)

    def look(owner):
        count = jnp.int32(0)
        tile = [jnp.int32(TILES), jnp.int32(TILES)]
        for t in range(TILES):
            hit = tile_owner_ref[t] == owner
            for r in range(CAP):
                tile[r] = jnp.where(jnp.logical_and(hit, count == r), t, tile[r])
            count = count + jnp.where(hit, 1, 0)
        for r in range(CAP):
            tab[owner * CAP + r] = tile[r] if r == 0 else tile[r] + 1 - 2 * lax.rem(tile[r], 2)

    def turn(u):
        fetch(u).wait()
        j, b = lax.div(u, BANDS), lax.rem(u, BANDS)
        rows = pl.ds(pl.multiple_of(b * BAND, BAND), BAND)
        block = jnp.swapaxes(half[1, j, :, rows, :], 0, 1)
        block = jnp.stack([block[m].T for m in range(BAND)], 0)
        flat[j, :, rows, :] = jnp.swapaxes(block, 0, 1)

    def turn_and_look(u):
        turn(u)
        look(u - 12)

    each(0, 6, turn)
    pl.semaphore_wait(barrier, NF - 1 + NA - 1)

    def hop1(i):
        peer = fit_peer(i)
        return pltpu.make_async_remote_copy(
            src_ref=own.at[peer], dst_ref=first.at[i], send_sem=s1.at[i], recv_sem=r1.at[i],
            device_id=(peer, ao), device_id_type=MESH)

    def hop2(i):
        return pltpu.make_async_remote_copy(
            src_ref=piece, dst_ref=second.at[i], send_sem=s2.at[i], recv_sem=r2.at[i],
            device_id=(fit, ao_peer(i)), device_id_type=MESH)

    def hop3(i):
        return pltpu.make_async_remote_copy(
            src_ref=both, dst_ref=done.at[i], send_sem=s3.at[i], recv_sem=r3.at[i],
            device_id=(fit_peer(i), ao), device_id_type=MESH)

    def hop_a(c, i):
        return pltpu.make_async_remote_copy(
            src_ref=send.at[c, i], dst_ref=recv.at[c, i], send_sem=sa.at[c, i], recv_sem=ra.at[c, i],
            device_id=(fit, ao_peer(i)), device_id_type=MESH)

    def hop_b(c, i):
        peer = fit_peer(i)
        return pltpu.make_async_remote_copy(
            src_ref=bsend.at[c, peer], dst_ref=brecv.at[c, i], send_sem=sb.at[c, i], recv_sem=rb.at[c, i],
            device_id=(peer, ao), device_id_type=MESH)

    every(1, NF, lambda i: hop1(i).start())
    each(6, 12, turn)

    every(1, NF, lambda i: hop1(i).wait_recv())
    total = own[fit].astype(F32)
    for i in range(1, NF):
        total = total + first[i].astype(F32)
    piece[...] = total.astype(BF16)
    every(1, NA, lambda i: hop2(i).start())

    each(0, NA, look)
    each(12, 22, turn)
    every(1, NA, lambda i: hop2(i).wait_recv())
    for i in range(1, NA):
        total = total + second[i].astype(F32)
    both[...] = total.astype(BF16)
    every(1, NF, lambda i: hop3(i).start())
    coeff[fit] = both[...]
    each(22, 32, turn)
    every(1, NF, lambda i: hop3(i).wait_recv())

    def put(i):
        coeff[lax.rem(fit + NF - i, NF)] = done[i]

    each(1, NF, put)

    pair = coeff[...].reshape(2, W, W)
    orbitals = jnp.concatenate([pair[0], pair[1]], 1)

    def product(v):
        j = lax.div(v, W // WIDE)
        some = pl.ds(pl.multiple_of(lax.rem(v, W // WIDE) * WIDE, WIDE), WIDE)
        r = jnp.dot(flat[j, some].reshape(WIDE * W, W), orbitals, preferred_element_type=F32)
        r = r.astype(BF16)
        half[0, j, some] = r[:, :W].reshape(WIDE, W, W)
        half[1, j, some] = r[:, W:].reshape(WIDE, W, W)

    each(0, MUB * W // WIDE, product)

    def rows_of(first, lo, n):
        return jnp.concatenate(
            [half[h, :, first + v, lo:lo + n, :].reshape(MUB * n, W)
             for h in range(2) for v in range(DEEP)], 1)

    head_row = lax.broadcasted_iota(jnp.int32, (HEAD, W), 0)

    def coded(tile):
        top = jnp.maximum(jnp.max(jnp.abs(tile), axis=0, keepdims=True), 1e-33)
        level = jnp.ceil(jnp.log2(top) * STEP)
        return jnp.round(tile * (TOP * jnp.exp2(level * (-1.0 / STEP)))), level.astype(jnp.int32)

    def narrow(values):
        return values.astype(jnp.int32).astype(I16)

    def decode_head(head):
        head = head.astype(jnp.int32).astype(F32)
        return jnp.exp2(head[0:1] * (1.0 / STEP)) * (1.0 / TOP), head[1:2]

    def decode(values):
        return values.astype(jnp.int32).astype(F32)

    left = lax.broadcasted_iota(jnp.int32, (CODED, W), 1) < ROWS
    left_row = left[:ROWS]
    sides[0] = jnp.where(left, -1, 0).astype(I16)
    sides[1] = jnp.where(left, 0, -1).astype(I16)

    def fill(p, i, where_to):
        owner = ao_peer(i)
        one, two = gram[p, tab[owner * CAP]], gram[p, tab[owner * CAP + 1]]
        where_to[p, i] = (one & sides[0]) | (two & sides[1])

    def store(p, t, tiles):
        keep = [
            jnp.full((1, W), (screen_ref[t // MUB] * screen_ref[n % MUB]).astype(F32), F32)
            for n in (t, t + 1)]
        values, level = coded(tiles * jnp.where(left_row[:1], keep[0], keep[1]))
        slot = jnp.where(left[:HEAD], tile_slot_ref[t], tile_slot_ref[t + 1])
        head = jnp.where(head_row == 0, level, slot)
        gram[p, t, pl.ds(0, ROWS)] = narrow(values)
        gram[p, t, pl.ds(ROWS, HEAD)] = head.astype(I16)
        gram[p, t + 1, pl.ds(0, ROWS)] = narrow(pltpu.roll(values, ROWS, 1))
        gram[p, t + 1, pl.ds(ROWS, HEAD)] = pltpu.roll(head, ROWS, 1).astype(I16)

    def share(p):
        for t in range(TILES, TILES + 2):
            gram[p, t] = jnp.full((CODED, W), -1, jnp.int32).astype(I16)

        def push(i):
            fill(p, i, send)
            hop_a(p, i).start()

        each(1, NA, push)
        fill(p, 0, recv)

    def block(stage, j, k):
        return acc[stage, j * ROWS:(j + 1) * ROWS, k // 2 * W:(k // 2 + 1) * W]

    for stage, (a, b) in enumerate(((0, 0), (0, 1), (1, 1))):
        acc[stage] = jnp.zeros((MUB * ROWS, MUB * ROWS), F32)

        def deep(i, stage=stage, a=a, b=b):
            one = rows_of(i * DEEP, a * ROWS, ROWS)
            two = one if a == b else rows_of(i * DEEP, b * ROWS, ROWS)
            acc[stage] += lax.dot_general(one, two, NT, preferred_element_type=F32)

        each(0, W // DEEP, deep)
        for j in range(MUB):
            for k in range(0, MUB, 2):
                store(a * 2 + b, j * MUB + k, block(stage, j, k))
        share(a * 2 + b)
        if a != b:
            for k in range(0, MUB, 2):
                for j in range(0, MUB, 2):
                    turned = jnp.concatenate([block(stage, k, j), block(stage, k + 1, j)], 0).T
                    store(2, j * MUB + k, turned[:ROWS])
                    store(2, (j + 1) * MUB + k, turned[ROWS:])
            share(2)

    order = (0, 1, 2, 3)
    for p in order:
        def heads(i, p=p):
            scale, slot = decode_head(recv[p, i, pl.ds(ROWS, HEAD)])
            scales[i] = jnp.broadcast_to(scale, (8, W))
            slots[i] = jnp.broadcast_to(slot, (8, W))

        def arrive(i, p=p, heads=heads):
            hop_a(p, i).wait_recv()
            heads(i)

        heads(0)
        each(1, NA, arrive)

        def band(b, p=p):
            for group in range(0, SLOTS, 8):
                def add(i, sums, group=group):
                    tile = decode(recv[p, i, pl.ds(b * 16, 16)]).reshape(2, 8, W) * scales[i][None]
                    slot = slots[i]
                    return [
                        sums[q] + jnp.where((slot == float(group + q))[None], tile, 0.0)
                        for q in range(8)]

                zero = jnp.zeros((2, 8, W), F32)
                sums = lax.fori_loop(0, NA, add, [zero] * 8, unroll=16)
                for q in range(0, 8, 2):
                    even, odd = sums[q].reshape(16, W), sums[q + 1].reshape(16, W)
                    swapped = pltpu.roll(jnp.where(left[:16], odd, even), ROWS, 1)
                    sums_of[(group + q) // 2, pl.ds(b * 16, 16)] = jnp.where(left[:16], even, odd) + swapped

        each(0, ROWS // 16, band)

        def pack(i, p=p):
            g = fit_peer(i)
            values, level = coded(sums_of[g])
            bsend[p, g, pl.ds(0, ROWS)] = narrow(values)
            bsend[p, g, pl.ds(ROWS, HEAD)] = jnp.where(head_row == 0, level, 0).astype(I16)
            hop_b(p, i).start()

        each(1, NF, pack)
        mine[p] = sums_of[fit]

    every(1, NF, lambda i: hop1(i).wait_send())
    every(1, NA, lambda i: hop2(i).wait_send())
    every(1, NF, lambda i: hop3(i).wait_send())
    for p in order:
        each(1, NA, lambda i, p=p: hop_a(p, i).wait_send())

    def fit_sum(p):
        each(1, NF, lambda i: hop_b(p, i).wait_recv())
        sums = mine[p]
        for i in range(1, NF):
            scale, _ = decode_head(brecv[p, i, pl.ds(ROWS, HEAD)])
            sums = sums + decode(brecv[p, i, pl.ds(0, ROWS)]) * scale
        return sums

    def leave(a):
        rows = pl.ds(a * ROWS, ROWS)
        return pltpu.make_async_copy(out_ref.at[:, rows], out_hbm.at[:, rows], small.at[a])

    for a in range(2):
        one, two = fit_sum(2 * a), fit_sum(2 * a + 1)
        rows = pl.ds(a * ROWS, ROWS)
        out_ref[0, rows] = jnp.where(left_row, one, pltpu.roll(two, ROWS, 1))
        out_ref[1, rows] = jnp.where(left_row, pltpu.roll(one, ROWS, 1), two)
        leave(a).start()

    for p in order:
        each(1, NF, lambda i, p=p: hop_b(p, i).wait_send())
    for a in range(2):
        leave(a).wait()


def on_device(three_index, occ_coeff, occ_owner, screen, tile_owner, tile_slot):
    dma = pltpu.SemaphoreType.DMA
    part = (PIECE, W)
    return pl.pallas_call(
        whole_kernel,
        out_shape=jax.ShapeDtypeStruct((2, W, W), F32),
        in_specs=[pl.BlockSpec(memory_space=pl.ANY)] * 6,
        out_specs=pl.BlockSpec(memory_space=pl.ANY),
        scratch_shapes=[
            pltpu.VMEM((2, W, W), F32),
            pltpu.SMEM((2,), jnp.int32),
            pltpu.SMEM((MUB,), jnp.int32),
            pltpu.SMEM((TILES,), jnp.int32),
            pltpu.SMEM((TILES,), jnp.int32),
            pltpu.VMEM((W, W), BF16),
            pltpu.VMEM((2, MUB, W, W, W), BF16),
            pltpu.VMEM((MUB, W, W, W), BF16),
            pltpu.VMEM((3, MUB * ROWS, MUB * ROWS), F32),
            pltpu.VMEM((PARTS, TILES + 2, CODED, W), I16),
            pltpu.VMEM((NF,) + part, BF16),
            pltpu.VMEM((NF,) + part, BF16),
            pltpu.VMEM(part, BF16),
            pltpu.VMEM((NA,) + part, BF16),
            pltpu.VMEM(part, BF16),
            pltpu.VMEM((NF,) + part, BF16),
            pltpu.VMEM((NF,) + part, BF16),
            pltpu.VMEM((NA, 8, W), F32),
            pltpu.VMEM((NA, 8, W), F32),
            pltpu.VMEM((PARTS, NA, CODED, W), I16),
            pltpu.VMEM((PARTS, NA, CODED, W), I16),
            pltpu.VMEM((NF, ROWS, W), F32),
            pltpu.VMEM((PARTS, ROWS, W), F32),
            pltpu.VMEM((2, CODED, W), I16),
            pltpu.VMEM((PARTS, NF, CODED, W), I16),
            pltpu.VMEM((PARTS, NF, CODED, W), I16),
            pltpu.SMEM((NA * CAP,), jnp.int32),
            dma((UNITS,)), dma((5,)),
            dma((NF,)), dma((NF,)), dma((NA,)), dma((NA,)), dma((NF,)), dma((NF,)),
            dma((PARTS, NA)), dma((PARTS, NA)), dma((PARTS, NF)), dma((PARTS, NF)),
        ],
        compiler_params=pltpu.CompilerParams(
            collective_id=0, has_side_effects=True, vmem_limit_bytes=63 << 20),
        name="exchange",
    )(occ_owner, screen[:, 0], tile_owner[:, 0], tile_slot, occ_coeff[0], three_index)


def solution(mesh):
    in_specs = (
        P("ao", None, None, "fit"),
        P(("fit", "ao"), None, None),
        P(),
        P("ao", "fit"),
        P(("fit", "ao"), None),
        P(("fit", "ao")),
    )
    out_specs = P(("fit", "ao"), None, None)
    return jax.shard_map(
        on_device, mesh=mesh, in_specs=in_specs, out_specs=out_specs, check_vma=False
    )
```

```python
import jax
import jax.numpy as jnp
from jax import lax
from jax.experimental import pallas as pl
from jax.experimental.pallas import tpu as pltpu
from jax.sharding import PartitionSpec as P

MESH = pl.DeviceIdType.MESH
F32, BF16 = jnp.float32, jnp.bfloat16
NF, NA, SIDE = 8, 16, 4
MUB, TILES, SLOTS, CAP = 4, 16, 16, 2
W = 128
ORB = 2 * W
PIECE = W // 4
PARTS = 4
ROWS = W // 2
BAND = 16
BANDS = W // BAND
UNITS = MUB * BANDS
WIDE = 128
DEEP = 64
I16 = jnp.int16
HEAD = 8
CODED = ROWS + HEAD
TOP = 32766.0
STEP = 16.0
NT = (((1,), (1,)), ((), ()))


def every(start, stop, body):
    for i in range(start, stop):
        body(i)


def each(start, stop, body):
    def step(i, carry):
        body(i)
        return carry

    lax.fori_loop(start, stop, step, 0)


def whole_kernel(
    owner_in, screen_in, tile_owner_in, tile_slot_in, occ_in, three_ref, out_hbm,
    out_ref, owner_ref, screen_ref, tile_owner_ref, tile_slot_ref, occ_ref,
    half, flat, acc, gram, own, first, piece, second, both, done, coeff,
    scales, slots, send, recv, sums_of, mine, sides, bsend, brecv, tab,
    load, small, s1, r1, s2, r2, s3, r3, sa, ra, sb, rb,
):
    fit, ao = lax.axis_index("fit"), lax.axis_index("ao")
    me = fit * NA + ao
    z, y = lax.div(ao, SIDE), lax.rem(ao, SIDE)

    def fit_peer(i):
        return lax.rem(fit + i, NF)

    def ao_peer(i):
        dz, dy = (i // SIDE, i % SIDE) if isinstance(i, int) else (lax.div(i, SIDE), lax.rem(i, SIDE))
        return lax.rem(z + dz, SIDE) * SIDE + lax.rem(y + dy, SIDE)

    def fetch(u):
        j, b = lax.div(u, BANDS), lax.rem(u, BANDS)
        rows = pl.ds(pl.multiple_of(b * BAND, BAND), BAND)
        return pltpu.make_async_copy(three_ref.at[j, :, rows], half.at[1, j, :, rows], load.at[u])

    smalls = [
        pltpu.make_async_copy(here, there, small.at[n])
        for n, (here, there) in enumerate((
            (owner_in, owner_ref), (occ_in, occ_ref), (tile_owner_in, tile_owner_ref),
            (tile_slot_in, tile_slot_ref), (screen_in, screen_ref)))]
    for copy in smalls:
        copy.start()
    each(0, UNITS, lambda u: fetch(u).start())

    barrier = pltpu.get_barrier_semaphore()

    def greet_fit(i):
        pl.semaphore_signal(barrier, inc=1, device_id=(fit_peer(i), ao), device_id_type=MESH)

    def greet_ao(i):
        pl.semaphore_signal(barrier, inc=1, device_id=(fit, ao_peer(i)), device_id_type=MESH)

    every(1, NF, greet_fit)
    every(1, NA, greet_ao)

    for copy in smalls:
        copy.wait()
    occ = occ_ref[...].astype(F32)
    for which in range(2):
        keep = jnp.where(owner_ref[which] == me, 1.0, 0.0).astype(F32)
        own[pl.ds(which * 4, 4)] = (occ * keep).astype(BF16).reshape(4, PIECE, W)

    def look(owner):
        count = jnp.int32(0)
        tile = [jnp.int32(TILES), jnp.int32(TILES)]
        for t in range(TILES):
            hit = tile_owner_ref[t] == owner
            for r in range(CAP):
                tile[r] = jnp.where(jnp.logical_and(hit, count == r), t, tile[r])
            count = count + jnp.where(hit, 1, 0)
        for r in range(CAP):
            tab[owner * CAP + r] = tile[r] if r == 0 else tile[r] + 1 - 2 * lax.rem(tile[r], 2)

    def turn(u):
        fetch(u).wait()
        j, b = lax.div(u, BANDS), lax.rem(u, BANDS)
        rows = pl.ds(pl.multiple_of(b * BAND, BAND), BAND)
        block = jnp.swapaxes(half[1, j, :, rows, :], 0, 1)
        block = jnp.stack([block[m].T for m in range(BAND)], 0)
        flat[j, :, rows, :] = jnp.swapaxes(block, 0, 1)

    def turn_and_look(u):
        turn(u)
        look(u - 12)

    each(0, 6, turn)
    pl.semaphore_wait(barrier, NF - 1 + NA - 1)

    def hop1(i):
        peer = fit_peer(i)
        return pltpu.make_async_remote_copy(
            src_ref=own.at[peer], dst_ref=first.at[i], send_sem=s1.at[i], recv_sem=r1.at[i],
            device_id=(peer, ao), device_id_type=MESH)

    def hop2(i):
        return pltpu.make_async_remote_copy(
            src_ref=piece, dst_ref=second.at[i], send_sem=s2.at[i], recv_sem=r2.at[i],
            device_id=(fit, ao_peer(i)), device_id_type=MESH)

    def hop3(i):
        return pltpu.make_async_remote_copy(
            src_ref=both, dst_ref=done.at[i], send_sem=s3.at[i], recv_sem=r3.at[i],
            device_id=(fit_peer(i), ao), device_id_type=MESH)

    def hop_a(c, i):
        return pltpu.make_async_remote_copy(
            src_ref=send.at[c, i], dst_ref=recv.at[c, i], send_sem=sa.at[c, i], recv_sem=ra.at[c, i],
            device_id=(fit, ao_peer(i)), device_id_type=MESH)

    def hop_b(c, i):
        peer = fit_peer(i)
        return pltpu.make_async_remote_copy(
            src_ref=bsend.at[c, peer], dst_ref=brecv.at[c, i], send_sem=sb.at[c, i], recv_sem=rb.at[c, i],
            device_id=(peer, ao), device_id_type=MESH)

    every(1, NF, lambda i: hop1(i).start())
    each(6, 12, turn)

    every(1, NF, lambda i: hop1(i).wait_recv())
    total = own[fit].astype(F32)
    for i in range(1, NF):
        total = total + first[i].astype(F32)
    piece[...] = total.astype(BF16)
    every(1, NA, lambda n: hop2(NA - n).start())

    each(0, NA, look)
    each(12, 22, turn)
    every(1, NA, lambda i: hop2(i).wait_recv())
    for i in range(1, NA):
        total = total + second[i].astype(F32)
    both[...] = total.astype(BF16)
    every(1, NF, lambda i: hop3(i).start())
    coeff[fit] = both[...]
    each(22, 32, turn)
    every(1, NF, lambda i: hop3(i).wait_recv())

    def put(i):
        coeff[lax.rem(fit + NF - i, NF)] = done[i]

    each(1, NF, put)

    pair = coeff[...].reshape(2, W, W)
    orbitals = jnp.concatenate([pair[0], pair[1]], 1)

    def product(v):
        j = lax.div(v, W // WIDE)
        some = pl.ds(pl.multiple_of(lax.rem(v, W // WIDE) * WIDE, WIDE), WIDE)
        r = jnp.dot(flat[j, some].reshape(WIDE * W, W), orbitals, preferred_element_type=F32)
        r = r.astype(BF16)
        half[0, j, some] = r[:, :W].reshape(WIDE, W, W)
        half[1, j, some] = r[:, W:].reshape(WIDE, W, W)

    each(0, MUB * W // WIDE, product)

    def rows_of(first, lo, n):
        return jnp.concatenate(
            [half[h, :, first + v, lo:lo + n, :].reshape(MUB * n, W)
             for h in range(2) for v in range(DEEP)], 1)

    head_row = lax.broadcasted_iota(jnp.int32, (HEAD, W), 0)

    def coded(tile):
        top = jnp.maximum(jnp.max(jnp.abs(tile), axis=0, keepdims=True), 1e-33)
        level = jnp.ceil(jnp.log2(top) * STEP)
        return jnp.round(tile * (TOP * jnp.exp2(level * (-1.0 / STEP)))), level.astype(jnp.int32)

    def narrow(values):
        return values.astype(jnp.int32).astype(I16)

    def decode_head(head):
        head = head.astype(jnp.int32).astype(F32)
        return jnp.exp2(head[0:1] * (1.0 / STEP)) * (1.0 / TOP), head[1:2]

    def decode(values):
        return values.astype(jnp.int32).astype(F32)

    left = lax.broadcasted_iota(jnp.int32, (CODED, W), 1) < ROWS
    left_row = left[:ROWS]
    sides[0] = jnp.where(left, -1, 0).astype(I16)
    sides[1] = jnp.where(left, 0, -1).astype(I16)

    def fill(p, i, where_to):
        owner = ao_peer(i)
        one, two = gram[p, tab[owner * CAP]], gram[p, tab[owner * CAP + 1]]
        where_to[p, i] = (one & sides[0]) | (two & sides[1])

    def store(p, t, tiles):
        keep = [
            jnp.full((1, W), (screen_ref[t // MUB] * screen_ref[n % MUB]).astype(F32), F32)
            for n in (t, t + 1)]
        values, level = coded(tiles * jnp.where(left_row[:1], keep[0], keep[1]))
        slot = jnp.where(left[:HEAD], tile_slot_ref[t], tile_slot_ref[t + 1])
        head = jnp.where(head_row == 0, level, slot)
        gram[p, t, pl.ds(0, ROWS)] = narrow(values)
        gram[p, t, pl.ds(ROWS, HEAD)] = head.astype(I16)
        gram[p, t + 1, pl.ds(0, ROWS)] = narrow(pltpu.roll(values, ROWS, 1))
        gram[p, t + 1, pl.ds(ROWS, HEAD)] = pltpu.roll(head, ROWS, 1).astype(I16)

    def share(p):
        for t in range(TILES, TILES + 2):
            gram[p, t] = jnp.full((CODED, W), -1, jnp.int32).astype(I16)

        def push(n):
            i = NA - n
            fill(p, i, send)
            hop_a(p, i).start()

        each(1, NA, push)
        fill(p, 0, recv)

    def block(stage, j, k):
        return acc[stage, j * ROWS:(j + 1) * ROWS, k // 2 * W:(k // 2 + 1) * W]

    for stage, (a, b) in enumerate(((0, 0), (0, 1), (1, 1))):
        acc[stage] = jnp.zeros((MUB * ROWS, MUB * ROWS), F32)

        def deep(i, stage=stage, a=a, b=b):
            one = rows_of(i * DEEP, a * ROWS, ROWS)
            two = one if a == b else rows_of(i * DEEP, b * ROWS, ROWS)
            acc[stage] += lax.dot_general(one, two, NT, preferred_element_type=F32)

        each(0, W // DEEP, deep)
        for j in range(MUB):
            for k in range(0, MUB, 2):
                store(a * 2 + b, j * MUB + k, block(stage, j, k))
        share(a * 2 + b)
        if a != b:
            for k in range(0, MUB, 2):
                for j in range(0, MUB, 2):
                    turned = jnp.concatenate([block(stage, k, j), block(stage, k + 1, j)], 0).T
                    store(2, j * MUB + k, turned[:ROWS])
                    store(2, (j + 1) * MUB + k, turned[ROWS:])
            share(2)

    order = (0, 1, 2, 3)
    for p in order:
        def heads(i, p=p):
            scale, slot = decode_head(recv[p, i, pl.ds(ROWS, HEAD)])
            scales[i] = jnp.broadcast_to(scale, (8, W))
            slots[i] = jnp.broadcast_to(slot, (8, W))

        def arrive(i, p=p, heads=heads):
            hop_a(p, i).wait_recv()
            heads(i)

        heads(0)
        each(1, NA, arrive)

        def band(b, p=p):
            for group in range(0, SLOTS, 8):
                def add(i, sums, group=group):
                    tile = decode(recv[p, i, pl.ds(b * 16, 16)]).reshape(2, 8, W) * scales[i][None]
                    slot = slots[i]
                    return [
                        sums[q] + jnp.where((slot == float(group + q))[None], tile, 0.0)
                        for q in range(8)]

                zero = jnp.zeros((2, 8, W), F32)
                sums = lax.fori_loop(0, NA, add, [zero] * 8, unroll=16)
                for q in range(0, 8, 2):
                    even, odd = sums[q].reshape(16, W), sums[q + 1].reshape(16, W)
                    swapped = pltpu.roll(jnp.where(left[:16], odd, even), ROWS, 1)
                    sums_of[(group + q) // 2, pl.ds(b * 16, 16)] = jnp.where(left[:16], even, odd) + swapped

        each(0, ROWS // 16, band)

        def pack(i, p=p):
            g = fit_peer(i)
            values, level = coded(sums_of[g])
            bsend[p, g, pl.ds(0, ROWS)] = narrow(values)
            bsend[p, g, pl.ds(ROWS, HEAD)] = jnp.where(head_row == 0, level, 0).astype(I16)
            hop_b(p, i).start()

        each(1, NF, pack)
        mine[p] = sums_of[fit]

    every(1, NF, lambda i: hop1(i).wait_send())
    every(1, NA, lambda i: hop2(i).wait_send())
    every(1, NF, lambda i: hop3(i).wait_send())
    for p in order:
        each(1, NA, lambda i, p=p: hop_a(p, i).wait_send())

    def fit_sum(p):
        each(1, NF, lambda i: hop_b(p, i).wait_recv())
        sums = mine[p]
        for i in range(1, NF):
            scale, _ = decode_head(brecv[p, i, pl.ds(ROWS, HEAD)])
            sums = sums + decode(brecv[p, i, pl.ds(0, ROWS)]) * scale
        return sums

    def leave(a):
        rows = pl.ds(a * ROWS, ROWS)
        return pltpu.make_async_copy(out_ref.at[:, rows], out_hbm.at[:, rows], small.at[a])

    for a in range(2):
        one, two = fit_sum(2 * a), fit_sum(2 * a + 1)
        rows = pl.ds(a * ROWS, ROWS)
        out_ref[0, rows] = jnp.where(left_row, one, pltpu.roll(two, ROWS, 1))
        out_ref[1, rows] = jnp.where(left_row, pltpu.roll(one, ROWS, 1), two)
        leave(a).start()

    for p in order:
        each(1, NF, lambda i, p=p: hop_b(p, i).wait_send())
    for a in range(2):
        leave(a).wait()


def on_device(three_index, occ_coeff, occ_owner, screen, tile_owner, tile_slot):
    dma = pltpu.SemaphoreType.DMA
    part = (PIECE, W)
    return pl.pallas_call(
        whole_kernel,
        out_shape=jax.ShapeDtypeStruct((2, W, W), F32),
        in_specs=[pl.BlockSpec(memory_space=pl.ANY)] * 6,
        out_specs=pl.BlockSpec(memory_space=pl.ANY),
        scratch_shapes=[
            pltpu.VMEM((2, W, W), F32),
            pltpu.SMEM((2,), jnp.int32),
            pltpu.SMEM((MUB,), jnp.int32),
            pltpu.SMEM((TILES,), jnp.int32),
            pltpu.SMEM((TILES,), jnp.int32),
            pltpu.VMEM((W, W), BF16),
            pltpu.VMEM((2, MUB, W, W, W), BF16),
            pltpu.VMEM((MUB, W, W, W), BF16),
            pltpu.VMEM((3, MUB * ROWS, MUB * ROWS), F32),
            pltpu.VMEM((PARTS, TILES + 2, CODED, W), I16),
            pltpu.VMEM((NF,) + part, BF16),
            pltpu.VMEM((NF,) + part, BF16),
            pltpu.VMEM(part, BF16),
            pltpu.VMEM((NA,) + part, BF16),
            pltpu.VMEM(part, BF16),
            pltpu.VMEM((NF,) + part, BF16),
            pltpu.VMEM((NF,) + part, BF16),
            pltpu.VMEM((NA, 8, W), F32),
            pltpu.VMEM((NA, 8, W), F32),
            pltpu.VMEM((PARTS, NA, CODED, W), I16),
            pltpu.VMEM((PARTS, NA, CODED, W), I16),
            pltpu.VMEM((NF, ROWS, W), F32),
            pltpu.VMEM((PARTS, ROWS, W), F32),
            pltpu.VMEM((2, CODED, W), I16),
            pltpu.VMEM((PARTS, NF, CODED, W), I16),
            pltpu.VMEM((PARTS, NF, CODED, W), I16),
            pltpu.SMEM((NA * CAP,), jnp.int32),
            dma((UNITS,)), dma((5,)),
            dma((NF,)), dma((NF,)), dma((NA,)), dma((NA,)), dma((NF,)), dma((NF,)),
            dma((PARTS, NA)), dma((PARTS, NA)), dma((PARTS, NF)), dma((PARTS, NF)),
        ],
        compiler_params=pltpu.CompilerParams(
            collective_id=0, has_side_effects=True, vmem_limit_bytes=63 << 20),
        name="exchange",
    )(occ_owner, screen[:, 0], tile_owner[:, 0], tile_slot, occ_coeff[0], three_index)


def solution(mesh):
    in_specs = (
        P("ao", None, None, "fit"),
        P(("fit", "ao"), None, None),
        P(),
        P("ao", "fit"),
        P(("fit", "ao"), None),
        P(("fit", "ao")),
    )
    out_specs = P(("fit", "ao"), None, None)
    return jax.shard_map(
        on_device, mesh=mesh, in_specs=in_specs, out_specs=out_specs, check_vma=False
    )
```

```python
import jax
import jax.numpy as jnp
from jax import lax
from jax.experimental import pallas as pl
from jax.experimental.pallas import tpu as pltpu
from jax.sharding import PartitionSpec as P

MESH = pl.DeviceIdType.MESH
F32, BF16 = jnp.float32, jnp.bfloat16
NF, NA, SIDE = 8, 16, 4
MUB, TILES, SLOTS, CAP = 4, 16, 16, 2
W = 128
ORB = 2 * W
PIECE = W // 4
PARTS = 4
FAR_FIRST = (4, 3, 5, 2, 6, 1, 7)
ROWS = W // 2
BAND = 16
BANDS = W // BAND
UNITS = MUB * BANDS
WIDE = 128
DEEP = 64
I16 = jnp.int16
HEAD = 8
CODED = ROWS + HEAD
TOP = 32766.0
STEP = 16.0
NT = (((1,), (1,)), ((), ()))


def every(start, stop, body):
    for i in range(start, stop):
        body(i)


def each(start, stop, body):
    def step(i, carry):
        body(i)
        return carry

    lax.fori_loop(start, stop, step, 0)


def whole_kernel(
    owner_in, screen_in, tile_owner_in, tile_slot_in, occ_in, three_ref, out_hbm,
    out_ref, owner_ref, screen_ref, tile_owner_ref, tile_slot_ref, occ_ref,
    half, flat, acc, gram, own, first, piece, second, both, done, coeff,
    scales, slots, send, recv, sums_of, mine, sides, bsend, brecv, tab,
    load, small, s1, r1, s2, r2, s3, r3, sa, ra, sb, rb,
):
    fit, ao = lax.axis_index("fit"), lax.axis_index("ao")
    me = fit * NA + ao
    z, y = lax.div(ao, SIDE), lax.rem(ao, SIDE)

    def fit_peer(i):
        return lax.rem(fit + i, NF)

    def ao_peer(i):
        dz, dy = (i // SIDE, i % SIDE) if isinstance(i, int) else (lax.div(i, SIDE), lax.rem(i, SIDE))
        return lax.rem(z + dz, SIDE) * SIDE + lax.rem(y + dy, SIDE)

    def fetch(u):
        j, b = lax.div(u, BANDS), lax.rem(u, BANDS)
        rows = pl.ds(pl.multiple_of(b * BAND, BAND), BAND)
        return pltpu.make_async_copy(three_ref.at[j, :, rows], half.at[1, j, :, rows], load.at[u])

    smalls = [
        pltpu.make_async_copy(here, there, small.at[n])
        for n, (here, there) in enumerate((
            (owner_in, owner_ref), (occ_in, occ_ref), (tile_owner_in, tile_owner_ref),
            (tile_slot_in, tile_slot_ref), (screen_in, screen_ref)))]
    for copy in smalls:
        copy.start()
    each(0, UNITS, lambda u: fetch(u).start())

    barrier = pltpu.get_barrier_semaphore()

    def greet_fit(i):
        pl.semaphore_signal(barrier, inc=1, device_id=(fit_peer(i), ao), device_id_type=MESH)

    def greet_ao(i):
        pl.semaphore_signal(barrier, inc=1, device_id=(fit, ao_peer(i)), device_id_type=MESH)

    every(1, NF, greet_fit)
    every(1, NA, greet_ao)

    for copy in smalls:
        copy.wait()
    occ = occ_ref[...].astype(F32)
    for which in range(2):
        keep = jnp.where(owner_ref[which] == me, 1.0, 0.0).astype(F32)
        own[pl.ds(which * 4, 4)] = (occ * keep).astype(BF16).reshape(4, PIECE, W)

    def look(owner):
        count = jnp.int32(0)
        tile = [jnp.int32(TILES), jnp.int32(TILES)]
        for t in range(TILES):
            hit = tile_owner_ref[t] == owner
            for r in range(CAP):
                tile[r] = jnp.where(jnp.logical_and(hit, count == r), t, tile[r])
            count = count + jnp.where(hit, 1, 0)
        for r in range(CAP):
            tab[owner * CAP + r] = tile[r] if r == 0 else tile[r] + 1 - 2 * lax.rem(tile[r], 2)

    def turn(u):
        fetch(u).wait()
        j, b = lax.div(u, BANDS), lax.rem(u, BANDS)
        rows = pl.ds(pl.multiple_of(b * BAND, BAND), BAND)
        block = jnp.swapaxes(half[1, j, :, rows, :], 0, 1)
        block = jnp.stack([block[m].T for m in range(BAND)], 0)
        flat[j, :, rows, :] = jnp.swapaxes(block, 0, 1)

    def turn_and_look(u):
        turn(u)
        look(u - 12)

    each(0, 6, turn)
    pl.semaphore_wait(barrier, NF - 1 + NA - 1)

    def hop1(i):
        peer = fit_peer(i)
        return pltpu.make_async_remote_copy(
            src_ref=own.at[peer], dst_ref=first.at[i], send_sem=s1.at[i], recv_sem=r1.at[i],
            device_id=(peer, ao), device_id_type=MESH)

    def hop2(i):
        return pltpu.make_async_remote_copy(
            src_ref=piece, dst_ref=second.at[i], send_sem=s2.at[i], recv_sem=r2.at[i],
            device_id=(fit, ao_peer(i)), device_id_type=MESH)

    def hop3(i):
        return pltpu.make_async_remote_copy(
            src_ref=both, dst_ref=done.at[i], send_sem=s3.at[i], recv_sem=r3.at[i],
            device_id=(fit_peer(i), ao), device_id_type=MESH)

    def hop_a(c, i):
        return pltpu.make_async_remote_copy(
            src_ref=send.at[c, i], dst_ref=recv.at[c, i], send_sem=sa.at[c, i], recv_sem=ra.at[c, i],
            device_id=(fit, ao_peer(i)), device_id_type=MESH)

    def hop_b(c, i):
        peer = fit_peer(i)
        return pltpu.make_async_remote_copy(
            src_ref=bsend.at[c, peer], dst_ref=brecv.at[c, i], send_sem=sb.at[c, i], recv_sem=rb.at[c, i],
            device_id=(peer, ao), device_id_type=MESH)

    for i in FAR_FIRST:
        hop1(i).start()
    each(6, 12, turn)

    every(1, NF, lambda i: hop1(i).wait_recv())
    total = own[fit].astype(F32)
    for i in range(1, NF):
        total = total + first[i].astype(F32)
    piece[...] = total.astype(BF16)
    every(1, NA, lambda n: hop2(NA - n).start())

    each(0, NA, look)
    each(12, 22, turn)
    every(1, NA, lambda i: hop2(i).wait_recv())
    for i in range(1, NA):
        total = total + second[i].astype(F32)
    both[...] = total.astype(BF16)
    for i in FAR_FIRST:
        hop3(i).start()
    coeff[fit] = both[...]
    each(22, 32, turn)
    every(1, NF, lambda i: hop3(i).wait_recv())

    def put(i):
        coeff[lax.rem(fit + NF - i, NF)] = done[i]

    each(1, NF, put)

    pair = coeff[...].reshape(2, W, W)
    orbitals = jnp.concatenate([pair[0], pair[1]], 1)

    def product(v):
        j = lax.div(v, W // WIDE)
        some = pl.ds(pl.multiple_of(lax.rem(v, W // WIDE) * WIDE, WIDE), WIDE)
        r = jnp.dot(flat[j, some].reshape(WIDE * W, W), orbitals, preferred_element_type=F32)
        r = r.astype(BF16)
        half[0, j, some] = r[:, :W].reshape(WIDE, W, W)
        half[1, j, some] = r[:, W:].reshape(WIDE, W, W)

    each(0, MUB * W // WIDE, product)

    def rows_of(first, lo, n):
        return jnp.concatenate(
            [half[h, :, first + v, lo:lo + n, :].reshape(MUB * n, W)
             for h in range(2) for v in range(DEEP)], 1)

    head_row = lax.broadcasted_iota(jnp.int32, (HEAD, W), 0)

    def coded(tile):
        top = jnp.maximum(jnp.max(jnp.abs(tile), axis=0, keepdims=True), 1e-33)
        level = jnp.ceil(jnp.log2(top) * STEP)
        return jnp.round(tile * (TOP * jnp.exp2(level * (-1.0 / STEP)))), level.astype(jnp.int32)

    def narrow(values):
        return values.astype(jnp.int32).astype(I16)

    def decode_head(head):
        head = head.astype(jnp.int32).astype(F32)
        return jnp.exp2(head[0:1] * (1.0 / STEP)) * (1.0 / TOP), head[1:2]

    def decode(values):
        return values.astype(jnp.int32).astype(F32)

    left = lax.broadcasted_iota(jnp.int32, (CODED, W), 1) < ROWS
    left_row = left[:ROWS]
    sides[0] = jnp.where(left, -1, 0).astype(I16)
    sides[1] = jnp.where(left, 0, -1).astype(I16)

    def fill(p, i, where_to):
        owner = ao_peer(i)
        one, two = gram[p, tab[owner * CAP]], gram[p, tab[owner * CAP + 1]]
        where_to[p, i] = (one & sides[0]) | (two & sides[1])

    def store(p, t, tiles):
        keep = [
            jnp.full((1, W), (screen_ref[t // MUB] * screen_ref[n % MUB]).astype(F32), F32)
            for n in (t, t + 1)]
        values, level = coded(tiles * jnp.where(left_row[:1], keep[0], keep[1]))
        slot = jnp.where(left[:HEAD], tile_slot_ref[t], tile_slot_ref[t + 1])
        head = jnp.where(head_row == 0, level, slot)
        gram[p, t, pl.ds(0, ROWS)] = narrow(values)
        gram[p, t, pl.ds(ROWS, HEAD)] = head.astype(I16)
        gram[p, t + 1, pl.ds(0, ROWS)] = narrow(pltpu.roll(values, ROWS, 1))
        gram[p, t + 1, pl.ds(ROWS, HEAD)] = pltpu.roll(head, ROWS, 1).astype(I16)

    def share(p):
        for t in range(TILES, TILES + 2):
            gram[p, t] = jnp.full((CODED, W), -1, jnp.int32).astype(I16)

        def push(n):
            i = NA - n
            fill(p, i, send)
            hop_a(p, i).start()

        each(1, NA, push)
        fill(p, 0, recv)

    def block(stage, j, k):
        return acc[stage, j * ROWS:(j + 1) * ROWS, k // 2 * W:(k // 2 + 1) * W]

    for stage, (a, b) in enumerate(((0, 0), (0, 1), (1, 1))):
        acc[stage] = jnp.zeros((MUB * ROWS, MUB * ROWS), F32)

        def deep(i, stage=stage, a=a, b=b):
            one = rows_of(i * DEEP, a * ROWS, ROWS)
            two = one if a == b else rows_of(i * DEEP, b * ROWS, ROWS)
            acc[stage] += lax.dot_general(one, two, NT, preferred_element_type=F32)

        each(0, W // DEEP, deep)
        for j in range(MUB):
            for k in range(0, MUB, 2):
                store(a * 2 + b, j * MUB + k, block(stage, j, k))
        share(a * 2 + b)
        if a != b:
            for k in range(0, MUB, 2):
                for j in range(0, MUB, 2):
                    turned = jnp.concatenate([block(stage, k, j), block(stage, k + 1, j)], 0).T
                    store(2, j * MUB + k, turned[:ROWS])
                    store(2, (j + 1) * MUB + k, turned[ROWS:])
            share(2)

    order = (0, 1, 2, 3)
    for p in order:
        def heads(i, p=p):
            scale, slot = decode_head(recv[p, i, pl.ds(ROWS, HEAD)])
            scales[i] = jnp.broadcast_to(scale, (8, W))
            slots[i] = jnp.broadcast_to(slot, (8, W))

        def arrive(i, p=p, heads=heads):
            hop_a(p, i).wait_recv()
            heads(i)

        heads(0)
        each(1, NA, arrive)

        def band(b, p=p):
            for group in range(0, SLOTS, 8):
                def add(i, sums, group=group):
                    tile = decode(recv[p, i, pl.ds(b * 16, 16)]).reshape(2, 8, W) * scales[i][None]
                    slot = slots[i]
                    return [
                        sums[q] + jnp.where((slot == float(group + q))[None], tile, 0.0)
                        for q in range(8)]

                zero = jnp.zeros((2, 8, W), F32)
                sums = lax.fori_loop(0, NA, add, [zero] * 8, unroll=16)
                for q in range(0, 8, 2):
                    even, odd = sums[q].reshape(16, W), sums[q + 1].reshape(16, W)
                    swapped = pltpu.roll(jnp.where(left[:16], odd, even), ROWS, 1)
                    sums_of[(group + q) // 2, pl.ds(b * 16, 16)] = jnp.where(left[:16], even, odd) + swapped

        each(0, ROWS // 16, band)

        def pack(i, p=p):
            g = fit_peer(i)
            values, level = coded(sums_of[g])
            bsend[p, g, pl.ds(0, ROWS)] = narrow(values)
            bsend[p, g, pl.ds(ROWS, HEAD)] = jnp.where(head_row == 0, level, 0).astype(I16)
            hop_b(p, i).start()

        each(1, NF, pack)
        mine[p] = sums_of[fit]

    every(1, NF, lambda i: hop1(i).wait_send())
    every(1, NA, lambda i: hop2(i).wait_send())
    every(1, NF, lambda i: hop3(i).wait_send())
    for p in order:
        each(1, NA, lambda i, p=p: hop_a(p, i).wait_send())

    def fit_sum(p):
        each(1, NF, lambda i: hop_b(p, i).wait_recv())
        sums = mine[p]
        for i in range(1, NF):
            scale, _ = decode_head(brecv[p, i, pl.ds(ROWS, HEAD)])
            sums = sums + decode(brecv[p, i, pl.ds(0, ROWS)]) * scale
        return sums

    def leave(a):
        rows = pl.ds(a * ROWS, ROWS)
        return pltpu.make_async_copy(out_ref.at[:, rows], out_hbm.at[:, rows], small.at[a])

    for a in range(2):
        one, two = fit_sum(2 * a), fit_sum(2 * a + 1)
        rows = pl.ds(a * ROWS, ROWS)
        out_ref[0, rows] = jnp.where(left_row, one, pltpu.roll(two, ROWS, 1))
        out_ref[1, rows] = jnp.where(left_row, pltpu.roll(one, ROWS, 1), two)
        leave(a).start()

    for p in order:
        each(1, NF, lambda i, p=p: hop_b(p, i).wait_send())
    for a in range(2):
        leave(a).wait()


def on_device(three_index, occ_coeff, occ_owner, screen, tile_owner, tile_slot):
    dma = pltpu.SemaphoreType.DMA
    part = (PIECE, W)
    return pl.pallas_call(
        whole_kernel,
        out_shape=jax.ShapeDtypeStruct((2, W, W), F32),
        in_specs=[pl.BlockSpec(memory_space=pl.ANY)] * 6,
        out_specs=pl.BlockSpec(memory_space=pl.ANY),
        scratch_shapes=[
            pltpu.VMEM((2, W, W), F32),
            pltpu.SMEM((2,), jnp.int32),
            pltpu.SMEM((MUB,), jnp.int32),
            pltpu.SMEM((TILES,), jnp.int32),
            pltpu.SMEM((TILES,), jnp.int32),
            pltpu.VMEM((W, W), BF16),
            pltpu.VMEM((2, MUB, W, W, W), BF16),
            pltpu.VMEM((MUB, W, W, W), BF16),
            pltpu.VMEM((3, MUB * ROWS, MUB * ROWS), F32),
            pltpu.VMEM((PARTS, TILES + 2, CODED, W), I16),
            pltpu.VMEM((NF,) + part, BF16),
            pltpu.VMEM((NF,) + part, BF16),
            pltpu.VMEM(part, BF16),
            pltpu.VMEM((NA,) + part, BF16),
            pltpu.VMEM(part, BF16),
            pltpu.VMEM((NF,) + part, BF16),
            pltpu.VMEM((NF,) + part, BF16),
            pltpu.VMEM((NA, 8, W), F32),
            pltpu.VMEM((NA, 8, W), F32),
            pltpu.VMEM((PARTS, NA, CODED, W), I16),
            pltpu.VMEM((PARTS, NA, CODED, W), I16),
            pltpu.VMEM((NF, ROWS, W), F32),
            pltpu.VMEM((PARTS, ROWS, W), F32),
            pltpu.VMEM((2, CODED, W), I16),
            pltpu.VMEM((PARTS, NF, CODED, W), I16),
            pltpu.VMEM((PARTS, NF, CODED, W), I16),
            pltpu.SMEM((NA * CAP,), jnp.int32),
            dma((UNITS,)), dma((5,)),
            dma((NF,)), dma((NF,)), dma((NA,)), dma((NA,)), dma((NF,)), dma((NF,)),
            dma((PARTS, NA)), dma((PARTS, NA)), dma((PARTS, NF)), dma((PARTS, NF)),
        ],
        compiler_params=pltpu.CompilerParams(
            collective_id=0, has_side_effects=True, vmem_limit_bytes=63 << 20),
        name="exchange",
    )(occ_owner, screen[:, 0], tile_owner[:, 0], tile_slot, occ_coeff[0], three_index)


def solution(mesh):
    in_specs = (
        P("ao", None, None, "fit"),
        P(("fit", "ao"), None, None),
        P(),
        P("ao", "fit"),
        P(("fit", "ao"), None),
        P(("fit", "ao")),
    )
    out_specs = P(("fit", "ao"), None, None)
    return jax.shard_map(
        on_device, mesh=mesh, in_specs=in_specs, out_specs=out_specs, check_vma=False
    )
```
